32 devices in a mesh: wa: 8 (over z, x), an: 4 (over y, core).
Axes of the slice: x: 2, y: 2, z: 4, core: 2. Of those that a mesh axis runs over, the one named last changes fastest.
Arguments:
- span_states: bfloat16 [192, 512, 640], P(('wa', 'an')), may hold values from -16 to 16
- offsets: int32 [192], P(('wa', 'an')), may hold values from 0 to 128, as said below
- lengths: int32 [192], P(('wa', 'an')), may hold values from 48 to 384, as said below
- cotangent: bfloat16 [192, 384, 640], P(('wa', 'an')), may hold values from -6 to 6
- qkv_weight: bfloat16 [1228800], P(('wa', 'an')), may hold values from -0.25 to 0.25
- out_weight: bfloat16 [409600], P(('wa', 'an')), may hold values from -1.25 to 1.25
- up_weight: bfloat16 [1638400], P(('wa', 'an')), may hold values from -0.25 to 0.25
- down_weight: bfloat16 [1638400], P(('wa', 'an')), may hold values from -0.125 to 0.125
- up_bias: bfloat16 [2560], P(('wa', 'an')), may hold values from -1.5 to 1.5
- norm_gains: bfloat16 [2, 640], P(None, 'wa'), may hold values from 0.5 to 1.5
- norm_shifts: bfloat16 [2, 640], P(None, 'wa'), may hold values from -1 to 1
- qkv_bias: bfloat16 [3, 640], P(None, 'wa'), may hold values from -1.5 to 1.5
- out_biases: bfloat16 [2, 640], P(None, 'wa'), may hold values from -1.5 to 1.5
Outputs:
- activations: bfloat16 [192, 384, 640], P(('wa', 'an'))
- span_grad: bfloat16 [192, 512, 640], P(('wa', 'an'))
- qkv_weight_grad: float32 [1228800], P(('wa', 'an'))
- out_weight_grad: float32 [409600], P(('wa', 'an'))
- up_weight_grad: float32 [1638400], P(('wa', 'an'))
- down_weight_grad: float32 [1638400], P(('wa', 'an'))
- up_bias_grad: float32 [2560], P(('wa', 'an'))
- norm_gains_grad: float32 [2, 640], P(None, 'wa')
- norm_shifts_grad: float32 [2, 640], P(None, 'wa')
- qkv_bias_grad: float32 [3, 640], P(None, 'wa')
- out_biases_grad: float32 [2, 640], P(None, 'wa')
- rms_values: float32 [3], replicated
The draws below stay inside these ranges and needn't reach their ends.
Inputs may be any that keep to these rules, and one draw needn't show every extreme that they name: `offsets`: A window whose offset is above 0 is full (length 384); some window starts at 128 in every draw. `lengths`: the valid tokens of a window are its first ones; some window is full in every draw.
All inputs are finite; a program needn't handle non-finite values.
Results may differ from the reference program's by a relative error of at most 0.0095.
Values may be sent and summed in bfloat16 or wider, within the bound.
No kernel may reach another device: no remote copies, remote signals or barrier semaphores. Data moves between devices by JAX's collectives and lax.ppermute only.
A program may use at most 256 MiB of HBM per device.

```python
import jax
import jax.numpy as jnp
from jax import lax

D = 640
HEADS = 20
FF = 2560
L = 384
CROP = 128
SPAN = 512
WINDOWS = 192


def window_plan(key):
    base_key = jax.random.fold_in(key, 4242)
    kind_key, share_key, jitter_key, start_key, pick_key = jax.random.split(base_key, 5)
    window_kinds = jax.random.randint(kind_key, (WINDOWS,), 0, 3)
    shares = jax.random.randint(share_key, (WINDOWS,), 0, 8)
    jitter = jax.random.randint(jitter_key, (WINDOWS,), 0, max(L // 16, 1))
    picked = jnp.arange(WINDOWS) == jax.random.randint(pick_key, (), 0, WINDOWS)
    cropped = (window_kinds == 0) | picked
    short_rows = jnp.minimum(L, L // (1 + shares) + jitter)
    window_lengths = jnp.where(cropped, L, short_rows).astype(jnp.int32)
    starts = jax.random.randint(start_key, (WINDOWS,), 0, CROP + 1)
    starts = jnp.where(picked, CROP, jnp.where(cropped, starts, 0)).astype(jnp.int32)
    return (starts, window_lengths)


def draw_offsets(key, part):
    return window_plan(key)[0]


def draw_lengths(key, part):
    return window_plan(key)[1]


def draw_span_states(key, part):
    rising = 3.0 ** (jnp.arange(WINDOWS, dtype=jnp.float32) / max(WINDOWS - 1, 1))
    noise = jax.random.truncated_normal(key, -5.0, 5.0, (WINDOWS, SPAN, D), jnp.float32)
    return (noise * rising[:, None, None]).astype(jnp.bfloat16)


def steps_of(key, shape, shards, smallest, largest):
    factor_of = 1.0
    for axis_at, blocks in shards:
        draws = jax.random.uniform(jax.random.fold_in(jax.random.fold_in(key, 6), axis_at), (blocks,), jnp.float32, smallest / len(shards), largest / len(shards))
        factor_of = factor_of * jnp.repeat(jnp.exp(draws), shape[axis_at] // blocks).reshape((-1,) + (1,) * (len(shape) - 1 - axis_at))
    return factor_of


def scatter_about(rng, shape, scale, reach, cuts=(), kind=jnp.bfloat16):
    values = jax.random.normal(rng, shape, jnp.float32) * scale
    if len(cuts) > 0:
        values = steps_of(rng, shape, cuts, -0.22, 0.18) * values
    return jnp.clip(values, min=-reach, max=reach).astype(kind)


def setup_inputs(seed: int = 0) -> dict:
    key_of = jax.random.split(jax.random.key(seed), 14)
    span_states = draw_span_states(jax.random.fold_in(key_of[13], 71), 0)
    offsets = draw_offsets(jax.random.fold_in(key_of[13], 71), 0)
    lengths = draw_lengths(jax.random.fold_in(key_of[13], 71), 0)
    cotangent = scatter_about(key_of[3], (WINDOWS, L, D), 1.0, 6.0, ((0, 32),))
    qkv_weight = scatter_about(key_of[4], (3 * D * D,), D ** -0.5, 0.25, ((0, 32),))
    out_weight = scatter_about(key_of[5], (D * D,), (D // 32) ** -0.5, 1.25, ((0, 32),))
    up_weight = scatter_about(key_of[6], (D * FF,), D ** -0.5, 0.25, ((0, 32),))
    down_weight = scatter_about(key_of[7], (FF * D,), FF ** -0.5, 0.125, ((0, 32),))
    up_bias = scatter_about(key_of[8], (FF,), 0.3, 1.5, ((0, 32),))
    norm_gains = jnp.clip(1.0 + 0.1 * jax.random.normal(key_of[9], (2, D), jnp.float32), 0.5, 1.5).astype(jnp.bfloat16)
    norm_shifts = scatter_about(key_of[10], (2, D), 0.2, 1.0, ((1, 8),))
    qkv_bias = scatter_about(key_of[11], (3, D), 0.3, 1.5, ((1, 8),))
    out_biases = scatter_about(key_of[12], (2, D), 0.3, 1.5, ((1, 8),))
    return {"span_states": span_states, "offsets": offsets, "lengths": lengths, "cotangent": cotangent, "qkv_weight": qkv_weight, "out_weight": out_weight, "up_weight": up_weight, "down_weight": down_weight, "up_bias": up_bias, "norm_gains": norm_gains, "norm_shifts": norm_shifts, "qkv_bias": qkv_bias, "out_biases": out_biases}


@jax.custom_vjp
def low(v):
    return lax.optimization_barrier(v.astype(jnp.bfloat16)).astype(jnp.float32)

@jax.custom_vjp
def low_back(v):
    return v

def low_keep(v):
    return (low(v), None)

def low_pass(kept, grad):
    return (grad,)

def back_keep(v):
    return (v, None)

def back_low(kept, grad):
    return (low(grad),)
low.defvjp(low_keep, low_pass)
low_back.defvjp(back_keep, back_low)

def matmul(left, right):
    return jnp.matmul(left, right, precision=lax.Precision.HIGHEST)

def layer_norm(values, gain, shift):
    mean_value = lax.optimization_barrier(jnp.mean(values, axis=-1, keepdims=True))
    centred = values - mean_value
    inverse = lax.rsqrt(lax.optimization_barrier(jnp.mean(centred * centred, axis=-1, keepdims=True)) + 1e-05)
    return centred * inverse * gain + shift

def rotate_half(values):
    middle_col = values.shape[-1] // 2
    return jnp.concatenate([-values[..., middle_col:], values[..., :middle_col]], axis=-1)

def rotary_tables(positions, width):
    inverse = 10000.0 ** (-jnp.arange(0, width, 2, dtype=jnp.float32) / width)
    angles = positions[..., None] * inverse
    angles = jnp.concatenate([angles, angles], axis=-1)
    return (jnp.cos(angles), jnp.sin(angles))

def rotate(values, cosine, sine):
    return values * cosine + rotate_half(values) * sine

def attend_window(pieces):
    queries, key_rows, value_rows, mask_row = pieces
    scores = jnp.einsum('qhd,khd->hqk', queries, key_rows, precision=lax.Precision.HIGHEST)
    scores = low_back(scores)
    scores = jnp.where(mask_row[None, None, :] > 0, scores, -1e+30)
    row_max = lax.optimization_barrier(jnp.max(scores, axis=-1, keepdims=True))
    raised = jnp.exp(scores - row_max)
    probs = low(raised / lax.optimization_barrier(jnp.sum(raised, axis=-1, keepdims=True)))
    return jnp.einsum('hqk,khd->qhd', probs, value_rows, precision=lax.Precision.HIGHEST)

def crop_window(span_one, start):
    return lax.dynamic_slice_in_dim(span_one, start.astype(jnp.int32), L, 0)

def forward(span_in, weights, starts, valid):
    w_qkv, w_out, w_up, w_down, bias_up, gains, shifts, bias_qkv, bias_out = weights
    windows = span_in.shape[0]
    width = D // HEADS
    inputs = jax.vmap(crop_window)(span_in, starts)
    normed_one = low(layer_norm(inputs, gains[0], shifts[0]))
    projected = low_back(matmul(normed_one, w_qkv) + bias_qkv.reshape(3 * D))
    positions = (starts[:, None] + jnp.arange(L, dtype=jnp.int32)[None, :]).astype(jnp.float32)
    cosine, sine = rotary_tables(positions, width)
    cosine = cosine[:, :, None, :]
    sine = sine[:, :, None, :]
    shaped = projected.reshape(windows, L, 3, HEADS, width)
    queries = low(rotate(shaped[:, :, 0] * width ** (-0.5), cosine, sine))
    key_rows = low(rotate(shaped[:, :, 1], cosine, sine))
    value_rows = low(shaped[:, :, 2])
    mixed = lax.map(jax.checkpoint(attend_window), (queries, key_rows, value_rows, valid))
    mixed = low(low_back(mixed.reshape(windows, L, D)))
    attn_out = low_back(matmul(mixed, w_out) + bias_out[0])
    middle = inputs + attn_out
    normed_two = low(layer_norm(middle, gains[1], shifts[1]))
    hidden_pre = low_back(matmul(normed_two, w_up) + bias_up)
    hidden = low(jax.nn.gelu(hidden_pre, approximate=False))
    ffn_out = low_back(matmul(hidden, w_down) + bias_out[1])
    result = middle + ffn_out

    def squares(values):
        return jnp.sum(valid * lax.optimization_barrier(jnp.sum(values * values, axis=-1)))
    return (result, jnp.stack([squares(result), squares(attn_out), squares(ffn_out)]))

def reference(span_states, offsets, lengths, cotangent, qkv_weight, out_weight, up_weight, down_weight, up_bias, norm_gains, norm_shifts, qkv_bias, out_biases):
    params = (qkv_weight.astype(jnp.float32).reshape(D, 3 * D), out_weight.astype(jnp.float32).reshape(D, D), up_weight.astype(jnp.float32).reshape(D, FF), down_weight.astype(jnp.float32).reshape(FF, D), up_bias.astype(jnp.float32), norm_gains.astype(jnp.float32), norm_shifts.astype(jnp.float32), qkv_bias.astype(jnp.float32), out_biases.astype(jnp.float32))
    group_size = 8
    group_count = WINDOWS // group_size
    spans = span_states.astype(jnp.float32).reshape(group_count, group_size, SPAN, D)
    start_rows = offsets.astype(jnp.int32).reshape(group_count, group_size)
    length_rows = lengths.astype(jnp.int32).reshape(group_count, group_size)
    cot_rows = cotangent.astype(jnp.float32).reshape(group_count, group_size, L, D)

    def step(carry, pieces):
        grad_sums, stat_sums = carry
        span_group, start_group, length_group, cot_group = pieces
        valid = (jnp.arange(L, dtype=jnp.int32)[None, :] < length_group[:, None]).astype(jnp.float32)

        def run(span_in, weights):
            return forward(span_in, weights, start_group, valid)
        result, backward, stats = jax.vjp(run, span_group, params, has_aux=True)
        grad_span, grad_params = backward(cot_group * valid[:, :, None])
        grad_sums = jax.tree.map(jnp.add, grad_sums, grad_params)
        return ((grad_sums, stat_sums + stats), (result.astype(jnp.bfloat16), grad_span.astype(jnp.bfloat16)))
    zero_grads = jax.tree.map(jnp.zeros_like, params)
    (grads, stat_sums), (results, span_grads) = lax.scan(step, (zero_grads, jnp.zeros((3,), jnp.float32)), (spans, start_rows, length_rows, cot_rows))
    token_count = jnp.sum(lengths).astype(jnp.float32)
    root_means = jnp.sqrt(stat_sums / (token_count * D))
    return (results.reshape(WINDOWS, L, D), span_grads.reshape(WINDOWS, SPAN, D), grads[0].reshape(3 * D * D), grads[1].reshape(D * D), grads[2].reshape(D * FF), grads[3].reshape(FF * D), grads[4], grads[5], grads[6], grads[7], grads[8], root_means)
```

```python
import math

import jax
import jax.numpy as jnp
from jax import lax
from jax.experimental import pallas as pl
from jax.experimental.pallas import tpu as pltpu
from jax.sharding import PartitionSpec as P

D = 640
HEADS = 20
FF = 2560
L = 384
CROP = 128
SPAN = L + CROP
HW = D // HEADS
LANES = 128
TILES = D // LANES
GROUP = LANES // HW
SCALE = HW**-0.5
F32 = jnp.float32
BF16 = jnp.bfloat16
BOTH = ("wa", "an")


def nn(a, b):
    return lax.dot_general(a, b, (((1,), (0,)), ((), ())), preferred_element_type=F32)


def nt(a, b):
    return lax.dot_general(a, b, (((1,), (1,)), ((), ())), preferred_element_type=F32)


def tn(a, b):
    return lax.dot_general(a, b, (((0,), (0,)), ((), ())), preferred_element_type=F32)


def lane_iota(rows, cols):
    return lax.broadcasted_iota(jnp.int32, (rows, cols), 1)


def normalize(v):
    centred = v - jnp.mean(v, axis=-1, keepdims=True)
    inverse = lax.rsqrt(jnp.mean(centred * centred, axis=-1, keepdims=True) + 1e-05)
    return centred * inverse, inverse


def norm_back(d, n, inverse):
    return inverse * (
        d - jnp.mean(d, axis=-1, keepdims=True) - n * jnp.mean(d * n, axis=-1, keepdims=True)
    )


def col_sum(v):
    return jnp.sum(v, axis=0, keepdims=True)


def split_lanes(v, last):
    high = v.astype(BF16).astype(F32)
    rest = v - high
    mid = rest.astype(BF16).astype(F32)
    low = rest - mid
    at = lane_iota(*v.shape) % HW
    out = jnp.where(at == 0, high, jnp.where(at == 1, mid, jnp.where(at == 2, low, 0.0)))
    return jnp.where(at == 3, last, out).astype(BF16)


def rolled(v):
    first = (lane_iota(*v.shape) % HW) < HW // 2
    ahead = pltpu.roll(v, LANES - HW // 2, 1)
    behind = pltpu.roll(v, HW // 2, 1)
    return jnp.where(first, ahead, behind)


def stack_heads(wide):
    head = (lane_iota(1, 2 * LANES) % LANES) // HW
    return [jnp.where(head == h, wide, jnp.zeros_like(wide)) for h in range(GROUP)]


def key_side(length):
    at = lane_iota(L, LANES) % HW
    row = lax.broadcasted_iota(jnp.int32, (L, LANES), 0)
    bias = jnp.where(row < length, 0.0, -1e30)
    return jnp.where(at < 3, 1.0, jnp.where(at == 3, bias, 0.0)).astype(BF16)


def take_rows(full, start):
    return pltpu.roll(full, (SPAN - start) % SPAN, 0)[:L]


def front_kernel(
    offsets, lengths, span, w_qkv, vecs, bias_qkv, cosine, sine,
    x_out, q_out, k_out, v_out, lse_out, mixed_out,
    proj, keys_big, values_big,
):
    window = pl.program_id(0)
    start = offsets[window]
    length = lengths[window]
    x = take_rows(span[0].astype(F32), start)
    x_out[0] = x.astype(BF16)
    n, _ = normalize(x)
    normed = (n * vecs[0:1, :] + vecs[1:2, :]).astype(BF16)
    proj[...] = nn(normed, w_qkv[...]) + bias_qkv[...]
    cos = take_rows(cosine[...], start)
    sin = take_rows(sine[...], start)
    for t in range(TILES):
        lanes = slice(t * LANES, (t + 1) * LANES)
        q = proj[:, t * LANES : (t + 1) * LANES] * SCALE
        q_out[0, t] = (q * cos + rolled(q) * sin).astype(BF16)
        k = proj[:, D + t * LANES : D + (t + 1) * LANES]
        k_out[0, t] = (k * cos + rolled(k) * sin).astype(BF16)
        v_out[0, t] = proj[:, 2 * D + t * LANES : 2 * D + (t + 1) * LANES].astype(BF16)

    key_lanes = key_side(length)
    ones = jnp.ones((L, LANES), BF16)
    query_lanes = jnp.where(lane_iota(LANES, LANES) % HW == 3, 1.0, 0.0).astype(BF16)
    head = lane_iota(LANES, LANES) // HW

    def tile(t, carry):
        for h, part in enumerate(stack_heads(jnp.concatenate([k_out[0, t], key_lanes], axis=1))):
            keys_big[h * L : (h + 1) * L, :] = part
        for h, part in enumerate(stack_heads(jnp.concatenate([v_out[0, t], ones], axis=1))):
            values_big[h * L : (h + 1) * L, :] = part
        for block in range(L // LANES):
            rows = slice(block * LANES, (block + 1) * LANES)
            queries = jnp.concatenate([q_out[0, t, rows, :], query_lanes], axis=1)
            raised = []
            tops = jnp.zeros((LANES, LANES), F32)
            for h in range(GROUP):
                scores = nt(queries, keys_big[h * L : (h + 1) * L, :])
                top = jnp.max(scores, axis=1, keepdims=True)
                raised.append(jnp.exp(scores - top).astype(BF16))
                tops = jnp.where(head == h, top, tops)
            sums = nn(jnp.concatenate(raised, axis=1), values_big[...])
            total = sums[:, LANES:]
            mixed_out[0, t, rows, :] = (sums[:, :LANES] / total).astype(BF16)
            lse_out[0, t, rows, :] = split_lanes(-(tops + jnp.log(total)), 1.0)
        return carry

    lax.fori_loop(0, TILES, tile, 0)


def middle_kernel(
    lengths, x_in, mixed_in, cotangent, w_out, w_up, w_down, vecs, bias_up,
    act_out, grad_mid_out, grad_mixed_out, dots_out,
    g_out, g_up, g_down, g_vecs, g_bias_up, stats,
    a_out, a_up, a_down, a_vecs, a_bias_up,
):
    window = pl.program_id(0)

    @pl.when(window == 0)
    def _():
        for ref in (a_out, a_up, a_down, a_vecs, a_bias_up, stats):
            ref[...] = jnp.zeros_like(ref)

    x = x_in[0].astype(F32)
    mixed = jnp.concatenate([mixed_in[0, t] for t in range(TILES)], axis=1)
    attn = nn(mixed, w_out[...]) + vecs[2:3, :]
    middle = x + attn
    n, inverse = normalize(middle)
    normed = (n * vecs[0:1, :] + vecs[1:2, :]).astype(BF16)
    row = lax.broadcasted_iota(jnp.int32, (L, 1), 0)
    valid = jnp.where(row < lengths[window], 1.0, 0.0)
    grad_result = cotangent[0].astype(F32) * valid
    grad_ffn = grad_result.astype(BF16)
    ffn = jnp.zeros((L, D), F32)
    grad_normed = jnp.zeros((L, D), F32)
    for c in range(FF // D):
        cols = slice(c * D, (c + 1) * D)
        up = w_up[:, cols]
        down = w_down[cols, :]
        pre = nn(normed, up) + bias_up[:, cols]
        phi = 0.5 + 0.5 * lax.erf(pre * math.sqrt(0.5))
        hidden = (pre * phi).astype(BF16)
        slope = phi + pre * (jnp.exp(-0.5 * pre * pre) * (1.0 / math.sqrt(2.0 * math.pi)))
        ffn = ffn + nn(hidden, down)
        grad_pre_f = nt(grad_ffn, down) * slope
        grad_pre = grad_pre_f.astype(BF16)
        a_up[:, cols] += tn(normed, grad_pre)
        a_down[cols, :] += tn(hidden, grad_ffn)
        a_bias_up[:, cols] += col_sum(grad_pre.astype(F32))
        grad_normed = grad_normed + nt(grad_pre, up)
    ffn = ffn + vecs[3:4, :]
    result = middle + ffn
    act_out[0] = result.astype(BF16)
    stats[0:1, :] += col_sum(valid * result * result)
    stats[1:2, :] += col_sum(valid * attn * attn)
    stats[2:3, :] += col_sum(valid * ffn * ffn)
    grad_middle = grad_result + norm_back(grad_normed * vecs[0:1, :], n, inverse)
    grad_mid_out[0] = grad_middle
    grad_attn = grad_middle.astype(BF16)
    a_out[...] += tn(mixed, grad_attn)
    a_vecs[0:1, :] += col_sum(grad_normed * n)
    a_vecs[1:2, :] += col_sum(grad_normed)
    a_vecs[2:3, :] += col_sum(grad_attn.astype(F32))
    a_vecs[3:4, :] += col_sum(grad_ffn.astype(F32))
    grad_mixed = nt(grad_attn, w_out[...]).astype(BF16)
    first = lax.broadcasted_iota(jnp.int32, (LANES, LANES), 0) // HW
    same = jnp.where(first == lane_iota(LANES, LANES) // HW, 1.0, 0.0).astype(BF16)
    for t in range(TILES):
        lanes = slice(t * LANES, (t + 1) * LANES)
        part = grad_mixed[:, lanes]
        grad_mixed_out[0, t] = part
        product = part.astype(F32) * mixed[:, lanes].astype(F32)
        high = product.astype(BF16)
        low = (product - high.astype(F32)).astype(BF16)
        dots_out[0, t] = split_lanes(-(nn(high, same) + nn(low, same)), 0.0)

    @pl.when(window == pl.num_programs(0) - 1)
    def _():
        g_out[...] = a_out[...].astype(g_out.dtype)
        g_up[...] = a_up[...].astype(g_up.dtype)
        g_down[...] = a_down[...].astype(g_down.dtype)
        g_vecs[...] = a_vecs[...]
        g_bias_up[...] = a_bias_up[...]


def back_kernel(
    offsets, lengths, x_in, q_in, k_in, v_in, lse_in, gm_in, dots_in, grad_mid, w_qkv, vecs,
    cosine, sine,
    span_grad, g_qkv, g_vecs, g_bias,
    a_qkv, grad_proj, queries_big, mixed_big, scores_back,
):
    window = pl.program_id(0)
    start = offsets[window]
    length = lengths[window]

    @pl.when(window == 0)
    def _():
        for ref in (a_qkv, g_vecs, g_bias):
            ref[...] = jnp.zeros_like(ref)

    cos = take_rows(cosine[...], start)
    sin = take_rows(sine[...], start)
    key_lanes = key_side(length)
    at = lane_iota(L, LANES) % HW
    value_lanes = jnp.where(at < 3, 1.0, 0.0).astype(BF16)
    for t in range(TILES):
        queries = jnp.concatenate([q_in[0, t], lse_in[0, t]], axis=1)
        for h, part in enumerate(stack_heads(queries)):
            queries_big[h * L : (h + 1) * L, :] = part
        mixed = jnp.concatenate([gm_in[0, t], dots_in[0, t]], axis=1)
        for h, part in enumerate(stack_heads(mixed)):
            mixed_big[h * L : (h + 1) * L, :] = part
        keys = jnp.concatenate([k_in[0, t], key_lanes], axis=1)
        values = jnp.concatenate([v_in[0, t], value_lanes], axis=1)
        for block in range(L // LANES):
            rows = slice(block * LANES, (block + 1) * LANES)
            low_probs = []
            for h in range(GROUP):
                part = slice(h * L, (h + 1) * L)
                probs = jnp.exp(nt(keys[rows, :], queries_big[part, :]))
                back = probs * nt(values[rows, :], mixed_big[part, :])
                scores_back[rows, h * L : (h + 1) * L] = back.astype(BF16)
                low_probs.append(probs.astype(BF16))
            grad_v = nn(jnp.concatenate(low_probs, axis=1), mixed_big[:, :LANES])
            grad_k = nn(scores_back[rows, :], queries_big[:, :LANES])
            grad_k = grad_k * cos[rows, :] - rolled(grad_k) * sin[rows, :]
            grad_proj[rows, D + t * LANES : D + (t + 1) * LANES] = grad_k.astype(BF16)
            grad_proj[rows, 2 * D + t * LANES : 2 * D + (t + 1) * LANES] = grad_v.astype(BF16)
        turned = nn(k_in[0, t].T, scores_back[...])
        grad_q = jnp.concatenate(
            [turned[h * HW : (h + 1) * HW, h * L : (h + 1) * L] for h in range(GROUP)], axis=0
        ).T
        grad_q = (grad_q * cos - rolled(grad_q) * sin) * SCALE
        grad_proj[:, t * LANES : (t + 1) * LANES] = grad_q.astype(BF16)
    x = x_in[0].astype(F32)
    n, inverse = normalize(x)
    normed = (n * vecs[0:1, :] + vecs[1:2, :]).astype(BF16)
    grads = grad_proj[...]
    a_qkv[...] += tn(normed, grads)
    g_bias[...] += col_sum(grads.astype(F32))
    grad_normed = nt(grads, w_qkv[...])
    g_vecs[0:1, :] += col_sum(grad_normed * n)
    g_vecs[1:2, :] += col_sum(grad_normed)
    grad_x = grad_mid[0] + norm_back(grad_normed * vecs[0:1, :], n, inverse)
    wide = jnp.concatenate([grad_x, jnp.zeros((CROP, D), F32)], axis=0)
    span_grad[0] = pltpu.roll(wide, start, 0).astype(BF16)

    @pl.when(window == pl.num_programs(0) - 1)
    def _():
        g_qkv[...] = a_qkv[...].astype(g_qkv.dtype)


def rows_spec(*dims):
    rank = len(dims)
    return pl.BlockSpec((1,) + dims, lambda w, *_: (w,) + (0,) * rank)


def whole_spec(*dims):
    rank = len(dims)
    return pl.BlockSpec(dims, lambda w, *_: (0,) * rank, pipeline_mode=pl.Buffered(1))


def call(kernel, scalars, windows, in_specs, outs, scratch, name):
    return pl.pallas_call(
        kernel,
        out_shape=[jax.ShapeDtypeStruct(shape, dtype) for _, shape, dtype in outs],
        grid_spec=pltpu.PrefetchScalarGridSpec(
            num_scalar_prefetch=scalars,
            grid=(windows,),
            in_specs=in_specs,
            out_specs=[spec for spec, _, _ in outs],
            scratch_shapes=scratch,
        ),
        compiler_params=pltpu.CompilerParams(
            dimension_semantics=("arbitrary",), vmem_limit_bytes=60 * 1024 * 1024
        ),
        name=name,
    )


def gather_rows(shard, cols, devices):
    if shard.shape[0] % cols == 0:
        full = lax.all_gather(shard.reshape(-1, cols), BOTH, axis=0, tiled=True)
        return full
    return lax.all_gather(shard, BOTH, axis=0, tiled=True).reshape(-1, cols)


def rotary_tables():
    inverse = 10000.0 ** (-jnp.arange(0, HW, 2, dtype=F32) / HW)
    angles = jnp.arange(SPAN, dtype=jnp.int32).astype(F32)[:, None] * inverse
    cosine = jnp.tile(jnp.cos(angles), (1, 2 * GROUP))
    sine = jnp.sin(angles)
    sine = jnp.tile(jnp.concatenate([-sine, sine], axis=1), (1, GROUP))
    return cosine, sine


def body(
    span_states,
    offsets,
    lengths,
    cotangent,
    qkv_weight,
    out_weight,
    up_weight,
    down_weight,
    up_bias,
    norm_gains,
    norm_shifts,
    qkv_bias,
    out_biases,
):
    windows = span_states.shape[0]
    wa, an = lax.axis_size("wa"), lax.axis_size("an")
    devices = wa * an
    w_qkv = gather_rows(qkv_weight, 3 * D, devices)
    rest = jnp.concatenate([out_weight, up_weight, down_weight])
    sizes = (out_weight.shape[0], up_weight.shape[0], down_weight.shape[0])
    wide = math.gcd(LANES, *sizes)
    rest = lax.all_gather(rest.reshape(-1, wide), BOTH, axis=0, tiled=False).reshape(devices, -1)
    w_out = rest[:, : sizes[0]].reshape(D, D)
    w_up = rest[:, sizes[0] : sizes[0] + sizes[1]].reshape(D, FF)
    w_down = rest[:, sizes[0] + sizes[1] :].reshape(FF, D)
    bias_up = lax.all_gather(up_bias, BOTH, axis=0, tiled=True).astype(F32).reshape(1, FF)
    small = jnp.concatenate([norm_gains, norm_shifts, qkv_bias, out_biases], axis=0)
    small = lax.all_gather(small, "wa", axis=1, tiled=True).astype(F32)
    vec_one = jnp.stack([small[0], small[2]])
    vec_two = jnp.stack([small[1], small[3], small[7], small[8]])
    bias_qkv = small[4:7].reshape(1, 3 * D)
    cosine, sine = rotary_tables()

    tiled_spec = rows_spec(TILES, L, LANES)
    tiled_shape = (windows, TILES, L, LANES)
    flat_spec = rows_spec(L, D)
    flat_shape = (windows, L, D)
    table_spec = whole_spec(SPAN, LANES)

    tiled_out = (tiled_spec, tiled_shape, BF16)
    x, q, k, v, lse, mixed = call(
        front_kernel,
        2,
        windows,
        [
            rows_spec(SPAN, D),
            whole_spec(D, 3 * D),
            whole_spec(2, D),
            whole_spec(1, 3 * D),
            table_spec,
            table_spec,
        ],
        [(flat_spec, flat_shape, BF16)] + [tiled_out] * 5,
        [
            pltpu.VMEM((L, 3 * D), F32),
            pltpu.VMEM((GROUP * L, 2 * LANES), BF16),
            pltpu.VMEM((GROUP * L, 2 * LANES), BF16),
        ],
        "front",
    )(offsets, lengths, span_states, w_qkv, vec_one, bias_qkv, cosine, sine)

    def kept(shape, dtype):
        return (whole_spec(*shape), shape, dtype)

    (
        activations,
        grad_mid,
        grad_mixed,
        dots,
        g_out,
        g_up,
        g_down,
        g_vec_two,
        g_bias_up,
        stats,
    ) = call(
        middle_kernel,
        1,
        windows,
        [
            flat_spec,
            tiled_spec,
            flat_spec,
            whole_spec(D, D),
            whole_spec(D, FF),
            whole_spec(FF, D),
            whole_spec(4, D),
            whole_spec(1, FF),
        ],
        [
            (flat_spec, flat_shape, BF16),
            (flat_spec, flat_shape, F32),
            tiled_out,
            tiled_out,
            kept((D, D), BF16),
            kept((D, FF), BF16),
            kept((FF, D), BF16),
            kept((4, D), F32),
            kept((1, FF), F32),
            kept((3, D), F32),
        ],
        [
            pltpu.VMEM((D, D), F32),
            pltpu.VMEM((D, FF), F32),
            pltpu.VMEM((FF, D), F32),
            pltpu.VMEM((4, D), F32),
            pltpu.VMEM((1, FF), F32),
        ],
        "middle",
    )(lengths, x, mixed, cotangent, w_out, w_up, w_down, vec_two, bias_up)

    grads = jnp.concatenate(
        [g.reshape(devices, -1, wide) for g in (g_out, g_up, g_down)], axis=1
    )
    rest_shard = lax.psum_scatter(grads, BOTH, scatter_dimension=0, tiled=False)
    rest_shard = rest_shard.reshape(-1).astype(F32)

    span_grad, g_qkv, g_vec_one, g_bias_qkv = call(
        back_kernel,
        2,
        windows,
        [flat_spec]
        + [tiled_spec] * 6
        + [flat_spec, whole_spec(D, 3 * D), whole_spec(2, D), table_spec, table_spec],
        [
            (rows_spec(SPAN, D), (windows, SPAN, D), BF16),
            kept((D, 3 * D), BF16),
            kept((2, D), F32),
            kept((1, 3 * D), F32),
        ],
        [
            pltpu.VMEM((D, 3 * D), F32),
            pltpu.VMEM((L, 3 * D), BF16),
            pltpu.VMEM((GROUP * L, 2 * LANES), BF16),
            pltpu.VMEM((GROUP * L, 2 * LANES), BF16),
            pltpu.VMEM((L, GROUP * L), BF16),
        ],
        "back",
    )(offsets, lengths, x, q, k, v, lse, grad_mixed, dots, grad_mid, w_qkv, vec_one, cosine, sine)

    qkv_shard = lax.psum_scatter(
        g_qkv.reshape(devices, -1, math.gcd(LANES, qkv_weight.shape[0])), BOTH, scatter_dimension=0, tiled=False
    )
    qkv_shard = qkv_shard.reshape(-1).astype(F32)

    token_count = jnp.sum(lengths).astype(F32)
    square = jnp.sum(stats, axis=1)
    tail = jnp.concatenate([square, token_count[None], jnp.zeros((D - 4,), F32)])
    packed = jnp.concatenate(
        [
            g_vec_one,
            g_vec_two,
            g_bias_qkv.reshape(3, D),
            g_bias_up.reshape(FF // D, D),
            tail[None],
        ],
        axis=0,
    )
    packed = lax.psum(packed, BOTH)
    share = D // wa
    first_col = lax.axis_index("wa") * share
    rows = packed[:9]
    rows = lax.dynamic_slice_in_dim(rows, first_col, share, 1)
    up_share = up_bias.shape[0]
    flat_index = lax.axis_index("wa") * an + lax.axis_index("an")
    up_bias_grad = lax.dynamic_slice_in_dim(
        packed[9:13].reshape(FF), flat_index * up_share, up_share, 0
    )
    totals = packed[13]
    root_means = jnp.sqrt(totals[:3] / (totals[3] * D))
    return (
        activations,
        span_grad,
        qkv_shard,
        rest_shard[: sizes[0]],
        rest_shard[sizes[0] : sizes[0] + sizes[1]],
        rest_shard[sizes[0] + sizes[1] :],
        up_bias_grad,
        jnp.stack([rows[0], rows[2]]),
        jnp.stack([rows[1], rows[3]]),
        rows[6:9],
        rows[4:6],
        root_means,
    )


def solution(mesh):
    return jax.shard_map(
        body,
        mesh=mesh,
        in_specs=(
            P(("wa", "an"), None, None),
            P(("wa", "an")),
            P(("wa", "an")),
            P(("wa", "an"), None, None),
            P(("wa", "an")),
            P(("wa", "an")),
            P(("wa", "an")),
            P(("wa", "an")),
            P(("wa", "an")),
            P(None, "wa"),
            P(None, "wa"),
            P(None, "wa"),
            P(None, "wa"),
        ),
        out_specs=(
            P(("wa", "an"), None, None),
            P(("wa", "an"), None, None),
            P(("wa", "an")),
            P(("wa", "an")),
            P(("wa", "an")),
            P(("wa", "an")),
            P(("wa", "an")),
            P(None, "wa"),
            P(None, "wa"),
            P(None, "wa"),
            P(None, "wa"),
            P(),
        ),
        check_vma=False,
    )
```

```python
import functools
import math

import jax
import jax.numpy as jnp
from jax import lax
from jax.experimental import pallas as pl
from jax.experimental.pallas import tpu as pltpu
from jax.sharding import PartitionSpec as P

D = 640
HEADS = 20
FF = 2560
L = 384
CROP = 128
SPAN = L + CROP
HW = D // HEADS
LANES = 128
TILES = D // LANES
GROUP = LANES // HW
SCALE = HW**-0.5
F32 = jnp.float32
BF16 = jnp.bfloat16
BOTH = ("wa", "an")


def nn(a, b):
    return lax.dot_general(a, b, (((1,), (0,)), ((), ())), preferred_element_type=F32)


def nt(a, b):
    return lax.dot_general(a, b, (((1,), (1,)), ((), ())), preferred_element_type=F32)


def tn(a, b):
    return lax.dot_general(a, b, (((0,), (0,)), ((), ())), preferred_element_type=F32)


def lane_iota(rows, cols):
    return lax.broadcasted_iota(jnp.int32, (rows, cols), 1)


def normalize(v):
    centred = v - jnp.mean(v, axis=-1, keepdims=True)
    inverse = lax.rsqrt(jnp.mean(centred * centred, axis=-1, keepdims=True) + 1e-05)
    return centred * inverse, inverse


def norm_back(d, n, inverse):
    return inverse * (
        d - jnp.mean(d, axis=-1, keepdims=True) - n * jnp.mean(d * n, axis=-1, keepdims=True)
    )


def col_sum(v):
    return jnp.sum(v, axis=0, keepdims=True)


def split_lanes(v, last):
    high = v.astype(BF16).astype(F32)
    rest = v - high
    mid = rest.astype(BF16).astype(F32)
    low = rest - mid
    at = lane_iota(*v.shape) % HW
    out = jnp.where(at == 0, high, jnp.where(at == 1, mid, jnp.where(at == 2, low, 0.0)))
    return jnp.where(at == 3, last, out).astype(BF16)


def rolled(v):
    first = (lane_iota(*v.shape) % HW) < HW // 2
    ahead = pltpu.roll(v, LANES - HW // 2, 1)
    behind = pltpu.roll(v, HW // 2, 1)
    return jnp.where(first, ahead, behind)


def stack_heads(wide):
    head = (lane_iota(1, 2 * LANES) % LANES) // HW
    return [jnp.where(head == h, wide, jnp.zeros_like(wide)) for h in range(GROUP)]


def key_side(length):
    at = lane_iota(L, LANES) % HW
    row = lax.broadcasted_iota(jnp.int32, (L, LANES), 0)
    bias = jnp.where(row < length, 0.0, -1e30)
    return jnp.where(at < 3, 1.0, jnp.where(at == 3, bias, 0.0)).astype(BF16)


def take_rows(full, start):
    return pltpu.roll(full, (SPAN - start) % SPAN, 0)[:L]


def unpack_rows(parts, rows, staging, dest):
    def group(i, carry):
        for ref, first, col, cols in parts:
            for j in range(4):
                low = first // 16 * 16
                high = min(-(-(first + rows) // 16) * 16, ref.shape[1])
                block = ref[4 * i + j, low:high, :].astype(F32)
                staging[j * rows : (j + 1) * rows, col : col + cols] = block[
                    first - low : first - low + rows
                ]
        at = pl.multiple_of(i * 4 * rows, 4 * rows)
        dest[pl.ds(at, 4 * rows), :] = staging[: 4 * rows, : dest.shape[1]].astype(BF16)
        return carry

    lax.fori_loop(0, dest.shape[0] // (4 * rows), group, 0)


def front_kernel(
    rows,
    offsets, lengths, span, w_first, w_second, vecs, bias_qkv, cosine, sine,
    x_out, q_out, k_out, v_out, lse_out, mixed_out, w_qkv,
    proj, keys_big, values_big, staging,
):
    window = pl.program_id(0)

    @pl.when(window == 0)
    def _():
        if rows:
            cut = w_first.shape[2]
            parts = [(w_first, 0, 0, cut), (w_second, 0, cut, 3 * D - cut)]
            unpack_rows(parts, rows, staging, w_qkv)
        else:
            w_qkv[:, : w_first.shape[1]] = w_first[...]
            w_qkv[:, w_first.shape[1] :] = w_second[...]

    start = offsets[window]
    length = lengths[window]
    x = take_rows(span[0].astype(F32), start)
    x_out[0] = x.astype(BF16)
    n, _ = normalize(x)
    normed = (n * vecs[0:1, :] + vecs[1:2, :]).astype(BF16)
    proj[...] = nn(normed, w_qkv[...]) + bias_qkv[...]
    cos = take_rows(cosine[...], start)
    sin = take_rows(sine[...], start)
    for t in range(TILES):
        lanes = slice(t * LANES, (t + 1) * LANES)
        q = proj[:, t * LANES : (t + 1) * LANES] * SCALE
        q_out[0, t] = (q * cos + rolled(q) * sin).astype(BF16)
        k = proj[:, D + t * LANES : D + (t + 1) * LANES]
        k_out[0, t] = (k * cos + rolled(k) * sin).astype(BF16)
        v_out[0, t] = proj[:, 2 * D + t * LANES : 2 * D + (t + 1) * LANES].astype(BF16)

    key_lanes = key_side(length)
    ones = jnp.ones((L, LANES), BF16)
    query_lanes = jnp.where(lane_iota(LANES, LANES) % HW == 3, 1.0, 0.0).astype(BF16)
    head = lane_iota(LANES, LANES) // HW

    def tile(t, carry):
        for h, part in enumerate(stack_heads(jnp.concatenate([k_out[0, t], key_lanes], axis=1))):
            keys_big[h * L : (h + 1) * L, :] = part
        for h, part in enumerate(stack_heads(jnp.concatenate([v_out[0, t], ones], axis=1))):
            values_big[h * L : (h + 1) * L, :] = part
        for block in range(L // LANES):
            part = slice(block * LANES, (block + 1) * LANES)
            queries = jnp.concatenate([q_out[0, t, part, :], query_lanes], axis=1)
            raised = []
            tops = jnp.zeros((LANES, LANES), F32)
            for h in range(GROUP):
                scores = nt(queries, keys_big[h * L : (h + 1) * L, :])
                top = jnp.max(scores, axis=1, keepdims=True)
                raised.append(jnp.exp(scores - top).astype(BF16))
                tops = jnp.where(head == h, top, tops)
            sums = nn(jnp.concatenate(raised, axis=1), values_big[...])
            total = sums[:, LANES:]
            mixed_out[0, t, part, :] = (sums[:, :LANES] / total).astype(BF16)
            lse_out[0, t, part, :] = split_lanes(-(tops + jnp.log(total)), 1.0)
        return carry

    lax.fori_loop(0, TILES, tile, 0)


def middle_kernel(
    rows,
    lengths, x_in, mixed_in, cotangent, packed, vecs, bias_up,
    act_out, grad_mid_out, grad_mixed_out, dots_out,
    g_packed, g_vecs, g_bias_up, stats,
    w_out, w_up, w_down, a_out, a_up, a_down, staging,
):
    window = pl.program_id(0)

    @pl.when(window == 0)
    def _():
        for ref in (a_out, a_up, a_down, g_vecs, g_bias_up, stats):
            ref[...] = jnp.zeros_like(ref)
        if rows:
            steps = FF // D

            def copy_down(i, carry):
                at = pl.multiple_of(i * steps * rows, steps * rows)
                w_down[pl.ds(at, steps * rows), :] = packed[i, : steps * rows, :]
                return carry

            lax.fori_loop(0, D // rows, copy_down, 0)
            parts = [(packed, (steps + c) * rows, c * D, D) for c in range(steps)]
            unpack_rows(parts, rows, staging, w_up)
            unpack_rows([(packed, 2 * steps * rows, 0, D)], rows, staging, w_out)
        else:
            w_down[...] = packed[:FF, :]
            for c in range(FF // D):
                w_up[:, c * D : (c + 1) * D] = packed[FF + c * D : FF + (c + 1) * D, :]
            w_out[...] = packed[2 * FF :, :]

    x = x_in[0].astype(F32)
    mixed = jnp.concatenate([mixed_in[0, t] for t in range(TILES)], axis=1)
    attn = nn(mixed, w_out[...]) + vecs[2:3, :]
    middle = x + attn
    n, inverse = normalize(middle)
    normed = (n * vecs[0:1, :] + vecs[1:2, :]).astype(BF16)
    row = lax.broadcasted_iota(jnp.int32, (L, 1), 0)
    valid = jnp.where(row < lengths[window], 1.0, 0.0)
    grad_result = cotangent[0].astype(F32) * valid
    grad_ffn = grad_result.astype(BF16)
    ffn = jnp.zeros((L, D), F32)
    grad_normed = jnp.zeros((L, D), F32)
    for c in range(FF // D):
        cols = slice(c * D, (c + 1) * D)
        up = w_up[:, cols]
        down = w_down[cols, :]
        pre = nn(normed, up) + bias_up[:, cols]
        phi = 0.5 + 0.5 * lax.erf(pre * math.sqrt(0.5))
        hidden = (pre * phi).astype(BF16)
        slope = phi + pre * (jnp.exp(-0.5 * pre * pre) * (1.0 / math.sqrt(2.0 * math.pi)))
        ffn = ffn + nn(hidden, down)
        grad_pre_f = nt(grad_ffn, down) * slope
        grad_pre = grad_pre_f.astype(BF16)
        a_up[:, cols] += tn(normed, grad_pre)
        a_down[cols, :] += tn(hidden, grad_ffn)
        g_bias_up[:, cols] += col_sum(grad_pre.astype(F32))
        grad_normed = grad_normed + nt(grad_pre, up)
    ffn = ffn + vecs[3:4, :]
    result = middle + ffn
    act_out[0] = result.astype(BF16)
    stats[0:1, :] += col_sum(valid * result * result)
    stats[1:2, :] += col_sum(valid * attn * attn)
    stats[2:3, :] += col_sum(valid * ffn * ffn)
    grad_middle = grad_result + norm_back(grad_normed * vecs[0:1, :], n, inverse)
    grad_mid_out[0] = grad_middle
    grad_attn = grad_middle.astype(BF16)
    a_out[...] += tn(mixed, grad_attn)
    g_vecs[0:1, :] += col_sum(grad_normed * n)
    g_vecs[1:2, :] += col_sum(grad_normed)
    g_vecs[2:3, :] += col_sum(grad_attn.astype(F32))
    g_vecs[3:4, :] += col_sum(grad_ffn.astype(F32))
    grad_mixed = nt(grad_attn, w_out[...]).astype(BF16)
    first = lax.broadcasted_iota(jnp.int32, (LANES, LANES), 0) // HW
    same = jnp.where(first == lane_iota(LANES, LANES) // HW, 1.0, 0.0).astype(BF16)
    for t in range(TILES):
        lanes = slice(t * LANES, (t + 1) * LANES)
        part = grad_mixed[:, lanes]
        grad_mixed_out[0, t] = part
        product = part.astype(F32) * mixed[:, lanes].astype(F32)
        high = product.astype(BF16)
        low = (product - high.astype(F32)).astype(BF16)
        dots_out[0, t] = split_lanes(-(nn(high, same) + nn(low, same)), 0.0)

    @pl.when(window == pl.num_programs(0) - 1)
    def _():
        steps = FF // D
        if rows:
            parts = [((steps + c) * rows, a_up, c * D) for c in range(steps)]
            parts.append((2 * steps * rows, a_out, 0))

            def group(i, carry):
                at = pl.multiple_of(i * 2 * rows, 2 * rows)
                for first, ref, col in parts:
                    block = ref[pl.ds(at, 2 * rows), col : col + D]
                    staging[first : first + rows, :D] = block[:rows]
                    staging[first : first + rows, D : 2 * D] = block[rows:]
                for j in range(2):
                    top = pl.multiple_of((2 * i + j) * steps * rows, steps * rows)
                    g_packed[2 * i + j, : steps * rows, :] = a_down[
                        pl.ds(top, steps * rows), :
                    ].astype(BF16)
                    g_packed[2 * i + j, steps * rows :, :] = staging[
                        steps * rows : g_packed.shape[1], j * D : (j + 1) * D
                    ].astype(BF16)
                return carry

            lax.fori_loop(0, D // (2 * rows), group, 0)
        else:
            g_packed[:FF, :] = a_down[...].astype(BF16)
            for c in range(steps):
                g_packed[FF + c * D : FF + (c + 1) * D, :] = a_up[
                    :, c * D : (c + 1) * D
                ].astype(BF16)
            g_packed[2 * FF :, :] = a_out[...].astype(BF16)


def back_kernel(
    rows,
    offsets, lengths, x_in, q_in, k_in, v_in, lse_in, gm_in, dots_in, grad_mid, w_qkv, vecs,
    cosine, sine,
    span_grad, g_first, g_second, g_vecs, g_bias,
    a_qkv, grad_proj, queries_big, mixed_big, scores_back,
):
    window = pl.program_id(0)
    start = offsets[window]
    length = lengths[window]

    @pl.when(window == 0)
    def _():
        for ref in (a_qkv, g_vecs, g_bias):
            ref[...] = jnp.zeros_like(ref)

    cos = take_rows(cosine[...], start)
    sin = take_rows(sine[...], start)
    key_lanes = key_side(length)
    at = lane_iota(L, LANES) % HW
    value_lanes = jnp.where(at < 3, 1.0, 0.0).astype(BF16)
    for t in range(TILES):
        queries = jnp.concatenate([q_in[0, t], lse_in[0, t]], axis=1)
        for h, part in enumerate(stack_heads(queries)):
            queries_big[h * L : (h + 1) * L, :] = part
        mixed = jnp.concatenate([gm_in[0, t], dots_in[0, t]], axis=1)
        for h, part in enumerate(stack_heads(mixed)):
            mixed_big[h * L : (h + 1) * L, :] = part
        keys = jnp.concatenate([k_in[0, t], key_lanes], axis=1)
        values = jnp.concatenate([v_in[0, t], value_lanes], axis=1)
        for block in range(L // LANES):
            here = slice(block * LANES, (block + 1) * LANES)
            low_probs = []
            for h in range(GROUP):
                heads = slice(h * L, (h + 1) * L)
                probs = jnp.exp(nt(keys[here, :], queries_big[heads, :]))
                back = probs * nt(values[here, :], mixed_big[heads, :])
                scores_back[here, h * L : (h + 1) * L] = back.astype(BF16)
                low_probs.append(probs.astype(BF16))
            grad_v = nn(jnp.concatenate(low_probs, axis=1), mixed_big[:, :LANES])
            grad_k = nn(scores_back[here, :], queries_big[:, :LANES])
            grad_k = grad_k * cos[here, :] - rolled(grad_k) * sin[here, :]
            grad_proj[here, D + t * LANES : D + (t + 1) * LANES] = grad_k.astype(BF16)
            grad_proj[here, 2 * D + t * LANES : 2 * D + (t + 1) * LANES] = grad_v.astype(BF16)
        turned = nn(k_in[0, t].T, scores_back[...])
        grad_q = jnp.concatenate(
            [turned[h * HW : (h + 1) * HW, h * L : (h + 1) * L] for h in range(GROUP)], axis=0
        ).T
        grad_q = (grad_q * cos - rolled(grad_q) * sin) * SCALE
        grad_proj[:, t * LANES : (t + 1) * LANES] = grad_q.astype(BF16)
    x = x_in[0].astype(F32)
    n, inverse = normalize(x)
    normed = (n * vecs[0:1, :] + vecs[1:2, :]).astype(BF16)
    grads = grad_proj[...]
    a_qkv[...] += tn(normed, grads)
    g_bias[...] += col_sum(grads.astype(F32))
    grad_normed = nt(grads, w_qkv[...])
    g_vecs[0:1, :] += col_sum(grad_normed * n)
    g_vecs[1:2, :] += col_sum(grad_normed)
    grad_x = grad_mid[0] + norm_back(grad_normed * vecs[0:1, :], n, inverse)
    wide = jnp.concatenate([grad_x, jnp.zeros((CROP, D), F32)], axis=0)
    span_grad[0] = pltpu.roll(wide, start, 0).astype(BF16)

    @pl.when(window == pl.num_programs(0) - 1)
    def _():
        cut = g_first.shape[-1]
        if rows:

            def group(i, carry):
                at = pl.multiple_of(i * 2 * rows, 2 * rows)
                block = a_qkv[pl.ds(at, 2 * rows), :]
                for j in range(2):
                    part = block[j * rows : (j + 1) * rows].astype(BF16)
                    g_first[2 * i + j] = part[:, :cut]
                    g_second[2 * i + j] = part[:, cut:]
                return carry

            lax.fori_loop(0, D // (2 * rows), group, 0)
        else:
            g_first[...] = a_qkv[:, :cut].astype(BF16)
            g_second[...] = a_qkv[:, cut:].astype(BF16)


def rows_spec(*dims):
    rank = len(dims)
    return pl.BlockSpec((1,) + dims, lambda w, *_: (w,) + (0,) * rank)


def whole_spec(*dims):
    rank = len(dims)
    return pl.BlockSpec(dims, lambda w, *_: (0,) * rank, pipeline_mode=pl.Buffered(1))


def call(kernel, scalars, windows, in_specs, outs, scratch, name):
    return pl.pallas_call(
        kernel,
        out_shape=[jax.ShapeDtypeStruct(shape, dtype) for _, shape, dtype in outs],
        grid_spec=pltpu.PrefetchScalarGridSpec(
            num_scalar_prefetch=scalars,
            grid=(windows,),
            in_specs=in_specs,
            out_specs=[spec for spec, _, _ in outs],
            scratch_shapes=scratch,
        ),
        compiler_params=pltpu.CompilerParams(
            dimension_semantics=("arbitrary",), vmem_limit_bytes=60 * 1024 * 1024
        ),
        name=name,
    )


def flat_index():
    return lax.axis_index("wa") * lax.axis_size("an") + lax.axis_index("an")


def swap(value, bit, devices):
    return lax.ppermute(value, BOTH, [(i, i ^ (1 << bit)) for i in range(devices)])


def gather_steps(shards, orders, devices):
    index = flat_index()
    done = [[] for _ in shards]
    values = list(shards)
    for step in range(len(orders[0])):
        for i, order in enumerate(orders):
            bit = order[step]
            mine = values[i]
            other = swap(mine, bit, devices)
            low = ((index >> bit) & 1) == 0
            axis = sum(1 for b in done[i] if b > bit)
            values[i] = jnp.stack(
                [jnp.where(low, mine, other), jnp.where(low, other, mine)], axis=axis
            )
            done[i].append(bit)
    return [v.reshape((devices,) + s.shape) for v, s in zip(values, shards)]


def scatter_steps(arrays, orders, devices):
    index = flat_index()
    bits = devices.bit_length() - 1
    left = [sorted(range(bits), reverse=True) for _ in arrays]
    values = [a.reshape((2,) * bits + a.shape[1:]) for a in arrays]
    for step in range(bits):
        for i, order in enumerate(orders):
            bit = order[step]
            axis = left[i].index(bit)
            own = (index >> bit) & 1
            send = lax.dynamic_index_in_dim(values[i], 1 - own, axis, keepdims=False)
            keep = lax.dynamic_index_in_dim(values[i], own, axis, keepdims=False)
            got = swap(send.astype(BF16), bit, devices)
            values[i] = keep.astype(F32) + got.astype(F32)
            left[i].remove(bit)
    return values


def sum_steps(value, devices):
    for bit in range(devices.bit_length() - 1):
        value = value + swap(value, bit, devices)
    return value


def rotary_tables():
    inverse = 10000.0 ** (-jnp.arange(0, HW, 2, dtype=F32) / HW)
    angles = jnp.arange(SPAN, dtype=jnp.int32).astype(F32)[:, None] * inverse
    cosine = jnp.tile(jnp.cos(angles), (1, 2 * GROUP))
    sine = jnp.sin(angles)
    sine = jnp.tile(jnp.concatenate([-sine, sine], axis=1), (1, GROUP))
    return cosine, sine


def body(
    span_states,
    offsets,
    lengths,
    cotangent,
    qkv_weight,
    out_weight,
    up_weight,
    down_weight,
    up_bias,
    norm_gains,
    norm_shifts,
    qkv_bias,
    out_biases,
):
    windows = span_states.shape[0]
    wa, an = lax.axis_size("wa"), lax.axis_size("an")
    devices = wa * an
    bits = devices.bit_length() - 1
    steps = FF // D
    rows = D // devices if D % (4 * devices) == 0 and devices == 1 << bits else 0
    cut = 8 * LANES
    small = jnp.concatenate([norm_gains, norm_shifts, qkv_bias, out_biases], axis=0)
    if rows:
        down_order = list(range(bits))[::-1]
        other_order = list(down_order)
        other_order[-2], other_order[-3] = other_order[-3], other_order[-2]
        shard = qkv_weight.reshape(rows, 3 * D)
        extra = jnp.concatenate([small, up_bias.reshape(1, -1)], axis=0)
        w_first, w_second, extra = gather_steps(
            [shard[:, :cut], shard[:, cut:], extra],
            [down_order, other_order, down_order],
            devices,
        )
        small = extra[::an, :-1].transpose(1, 0, 2).reshape(9, D).astype(F32)
        bias_up = extra[:, -1].astype(F32).reshape(1, FF)
        up = up_weight.reshape(rows, steps, D).transpose(1, 0, 2).reshape(steps * rows, D)
        pack_rows = -(-(2 * steps + 1) * rows // 32) * 32
        pad = jnp.zeros((pack_rows - (2 * steps + 1) * rows, D), BF16)
        packed = jnp.concatenate([down_weight.reshape(-1, D), up, out_weight.reshape(-1, D), pad])
        packed = lax.all_gather(packed, BOTH, axis=0, tiled=False)
    else:
        w_qkv = lax.all_gather(qkv_weight, BOTH, axis=0, tiled=True).reshape(D, 3 * D)
        w_first, w_second = w_qkv[:, :cut], w_qkv[:, cut:]
        small = lax.all_gather(small, "wa", axis=1, tiled=True).astype(F32)
        bias_up = lax.all_gather(up_bias, BOTH, axis=0, tiled=True).astype(F32).reshape(1, FF)
        w_down = lax.all_gather(down_weight, BOTH, axis=0, tiled=True).reshape(FF, D)
        w_up = lax.all_gather(up_weight, BOTH, axis=0, tiled=True)
        w_up = w_up.reshape(D, steps, D).transpose(1, 0, 2).reshape(FF, D)
        w_out = lax.all_gather(out_weight, BOTH, axis=0, tiled=True).reshape(D, D)
        packed = jnp.concatenate([w_down, w_up, w_out], axis=0)
    vec_one = jnp.stack([small[0], small[2]])
    vec_two = jnp.stack([small[1], small[3], small[7], small[8]])
    bias_qkv = small[4:7].reshape(1, 3 * D)
    cosine, sine = rotary_tables()

    tiled_spec = rows_spec(TILES, L, LANES)
    tiled_shape = (windows, TILES, L, LANES)
    flat_spec = rows_spec(L, D)
    flat_shape = (windows, L, D)
    table_spec = whole_spec(SPAN, LANES)

    tiled_out = (tiled_spec, tiled_shape, BF16)

    def kept(shape, dtype):
        return (whole_spec(*shape), shape, dtype)

    x, q, k, v, lse, mixed, w_qkv = call(
        functools.partial(front_kernel, rows),
        2,
        windows,
        [
            rows_spec(SPAN, D),
            whole_spec(*w_first.shape),
            whole_spec(*w_second.shape),
            whole_spec(2, D),
            whole_spec(1, 3 * D),
            table_spec,
            table_spec,
        ],
        [(flat_spec, flat_shape, BF16)] + [tiled_out] * 5 + [kept((D, 3 * D), BF16)],
        [
            pltpu.VMEM((L, 3 * D), F32),
            pltpu.VMEM((GROUP * L, 2 * LANES), BF16),
            pltpu.VMEM((GROUP * L, 2 * LANES), BF16),
            pltpu.VMEM((max(4 * rows, 8), 3 * D), F32),
        ],
        "front",
    )(offsets, lengths, span_states, w_first, w_second, vec_one, bias_qkv, cosine, sine)

    activations, grad_mid, grad_mixed, dots, g_packed, g_vec_two, g_bias_up, stats = call(
        functools.partial(middle_kernel, rows),
        1,
        windows,
        [
            flat_spec,
            tiled_spec,
            flat_spec,
            whole_spec(*packed.shape),
            whole_spec(4, D),
            whole_spec(1, FF),
        ],
        [
            (flat_spec, flat_shape, BF16),
            (flat_spec, flat_shape, F32),
            tiled_out,
            tiled_out,
            kept(packed.shape, BF16),
            kept((4, D), F32),
            kept((1, FF), F32),
            kept((3, D), F32),
        ],
        [
            pltpu.VMEM((D, D), BF16),
            pltpu.VMEM((D, FF), BF16),
            pltpu.VMEM((FF, D), BF16),
            pltpu.VMEM((D, D), F32),
            pltpu.VMEM((D, FF), F32),
            pltpu.VMEM((FF, D), F32),
            pltpu.VMEM((packed.shape[1] if rows else 8, FF), F32),
        ],
        "middle",
    )(lengths, x, mixed, cotangent, packed, vec_two, bias_up)

    if rows:
        packed_shard = lax.psum_scatter(g_packed, BOTH, scatter_dimension=0, tiled=False)
        packed_shard = packed_shard.astype(F32)
        down_grad = packed_shard[: steps * rows].reshape(-1)
        up_grad = packed_shard[steps * rows : 2 * steps * rows].reshape(steps, rows, D)
        up_grad = up_grad.transpose(1, 0, 2).reshape(-1)
        out_grad = packed_shard[2 * steps * rows : (2 * steps + 1) * rows].reshape(-1)
    else:

        def scatter_flat(grad):
            flat = grad.reshape(devices, -1)
            return lax.psum_scatter(flat, BOTH, scatter_dimension=0, tiled=False).astype(F32)

        down_grad = scatter_flat(g_packed[:FF])
        g_up = g_packed[FF : 2 * FF].reshape(steps, D, D).transpose(1, 0, 2)
        up_grad = scatter_flat(g_up)
        out_grad = scatter_flat(g_packed[2 * FF :])

    span_grad, g_first, g_second, g_vec_one, g_bias_qkv = call(
        functools.partial(back_kernel, rows),
        2,
        windows,
        [flat_spec]
        + [tiled_spec] * 6
        + [flat_spec, whole_spec(D, 3 * D), whole_spec(2, D), table_spec, table_spec],
        [
            (rows_spec(SPAN, D), (windows, SPAN, D), BF16),
            kept(w_first.shape, BF16),
            kept(w_second.shape, BF16),
            kept((2, D), F32),
            kept((1, 3 * D), F32),
        ],
        [
            pltpu.VMEM((D, 3 * D), F32),
            pltpu.VMEM((L, 3 * D), BF16),
            pltpu.VMEM((GROUP * L, 2 * LANES), BF16),
            pltpu.VMEM((GROUP * L, 2 * LANES), BF16),
            pltpu.VMEM((L, GROUP * L), BF16),
        ],
        "back",
    )(offsets, lengths, x, q, k, v, lse, grad_mixed, dots, grad_mid, w_qkv, vec_one, cosine, sine)

    if rows:
        g_first, g_second = scatter_steps(
            [g_first, g_second], [down_order[::-1], other_order[::-1]], devices
        )
        qkv_grad = jnp.concatenate([g_first, g_second], axis=1).reshape(-1)
    else:
        qkv_grad = scatter_flat(jnp.concatenate([g_first, g_second], axis=1))

    token_count = jnp.sum(lengths).astype(F32)
    square = jnp.sum(stats, axis=1)
    tail = jnp.concatenate([square, token_count[None], jnp.zeros((D - 4,), F32)])
    packed = jnp.concatenate(
        [
            g_vec_one,
            g_vec_two,
            g_bias_qkv.reshape(3, D),
            g_bias_up.reshape(FF // D, D),
            tail[None],
        ],
        axis=0,
    )
    packed = sum_steps(packed, devices) if rows else lax.psum(packed, BOTH)
    share = D // wa
    first_col = lax.axis_index("wa") * share
    shares = lax.dynamic_slice_in_dim(packed[:9], first_col, share, 1)
    up_share = up_bias.shape[0]
    up_bias_grad = lax.dynamic_slice_in_dim(
        packed[9:13].reshape(FF), flat_index() * up_share, up_share, 0
    )
    totals = packed[13]
    root_means = jnp.sqrt(totals[:3] / (totals[3] * D))
    return (
        activations,
        span_grad,
        qkv_grad,
        out_grad,
        up_grad,
        down_grad,
        up_bias_grad,
        jnp.stack([shares[0], shares[2]]),
        jnp.stack([shares[1], shares[3]]),
        shares[6:9],
        shares[4:6],
        root_means,
    )


def solution(mesh):
    return jax.shard_map(
        body,
        mesh=mesh,
        in_specs=(
            P(("wa", "an"), None, None),
            P(("wa", "an")),
            P(("wa", "an")),
            P(("wa", "an"), None, None),
            P(("wa", "an")),
            P(("wa", "an")),
            P(("wa", "an")),
            P(("wa", "an")),
            P(("wa", "an")),
            P(None, "wa"),
            P(None, "wa"),
            P(None, "wa"),
            P(None, "wa"),
        ),
        out_specs=(
            P(("wa", "an"), None, None),
            P(("wa", "an"), None, None),
            P(("wa", "an")),
            P(("wa", "an")),
            P(("wa", "an")),
            P(("wa", "an")),
            P(("wa", "an")),
            P(None, "wa"),
            P(None, "wa"),
            P(None, "wa"),
            P(None, "wa"),
            P(),
        ),
        check_vma=False,
    )
```

```python
import functools
import math

import jax
import jax.numpy as jnp
from jax import lax
from jax.experimental import pallas as pl
from jax.experimental.pallas import tpu as pltpu
from jax.sharding import PartitionSpec as P

D = 640
HEADS = 20
FF = 2560
L = 384
CROP = 128
SPAN = L + CROP
HW = D // HEADS
LANES = 128
TILES = D // LANES
GROUP = LANES // HW
SCALE = HW**-0.5
CHUNK = 512
F32 = jnp.float32
BF16 = jnp.bfloat16
BOTH = ("wa", "an")


def nn(a, b):
    return lax.dot_general(a, b, (((1,), (0,)), ((), ())), preferred_element_type=F32)


def nt(a, b):
    return lax.dot_general(a, b, (((1,), (1,)), ((), ())), preferred_element_type=F32)


def tn(a, b):
    return lax.dot_general(a, b, (((0,), (0,)), ((), ())), preferred_element_type=F32)


def lane_iota(rows, cols):
    return lax.broadcasted_iota(jnp.int32, (rows, cols), 1)


def normalize(v):
    centred = v - jnp.mean(v, axis=-1, keepdims=True)
    inverse = lax.rsqrt(jnp.mean(centred * centred, axis=-1, keepdims=True) + 1e-05)
    return centred * inverse, inverse


def norm_back(d, n, inverse):
    return inverse * (
        d - jnp.mean(d, axis=-1, keepdims=True) - n * jnp.mean(d * n, axis=-1, keepdims=True)
    )


def col_sum(v):
    return jnp.sum(v, axis=0, keepdims=True)


def split_lanes(v, last):
    high = v.astype(BF16).astype(F32)
    rest = v - high
    mid = rest.astype(BF16).astype(F32)
    low = rest - mid
    at = lane_iota(*v.shape) % HW
    out = jnp.where(at == 0, high, jnp.where(at == 1, mid, jnp.where(at == 2, low, 0.0)))
    return jnp.where(at == 3, last, out).astype(BF16)


def rolled(v):
    first = (lane_iota(*v.shape) % HW) < HW // 2
    ahead = pltpu.roll(v, LANES - HW // 2, 1)
    behind = pltpu.roll(v, HW // 2, 1)
    return jnp.where(first, ahead, behind)


def stack_heads(wide):
    head = (lane_iota(1, 2 * LANES) % LANES) // HW
    return [jnp.where(head == h, wide, jnp.zeros_like(wide)) for h in range(GROUP)]


def key_side(length):
    at = lane_iota(L, LANES) % HW
    row = lax.broadcasted_iota(jnp.int32, (L, LANES), 0)
    bias = jnp.where(row < length, 0.0, -1e30)
    return jnp.where(at < 3, 1.0, jnp.where(at == 3, bias, 0.0)).astype(BF16)


def take_rows(full, start):
    return pltpu.roll(full, (SPAN - start) % SPAN, 0)[:L]


def unpack_rows(parts, rows, staging, dest):
    def group(i, carry):
        for ref, first, col, cols in parts:
            for j in range(4):
                low = first // 16 * 16
                high = min(-(-(first + rows) // 16) * 16, ref.shape[1])
                block = ref[4 * i + j, low:high, :].astype(F32)
                staging[j * rows : (j + 1) * rows, col : col + cols] = block[
                    first - low : first - low + rows
                ]
        at = pl.multiple_of(i * 4 * rows, 4 * rows)
        dest[pl.ds(at, 4 * rows), :] = staging[: 4 * rows, : dest.shape[1]].astype(BF16)
        return carry

    lax.fori_loop(0, dest.shape[0] // (4 * rows), group, 0)


def front_kernel(
    rows,
    offsets, lengths, span, w_first, w_second, vecs, bias_qkv, cosine, sine,
    x_out, q_out, k_out, v_out, lse_out, mixed_out, w_qkv,
    proj, keys_big, values_big, staging,
):
    window = pl.program_id(0)

    @pl.when(window == 0)
    def _():
        if rows:
            cut = w_first.shape[2]
            parts = [(w_first, 0, 0, cut), (w_second, 0, cut, 3 * D - cut)]
            unpack_rows(parts, rows, staging, w_qkv)
        else:
            w_qkv[:, : w_first.shape[1]] = w_first[...]
            w_qkv[:, w_first.shape[1] :] = w_second[...]

    start = offsets[window]
    length = lengths[window]
    x = take_rows(span[0].astype(F32), start)
    x_out[0] = x.astype(BF16)
    n, _ = normalize(x)
    normed = (n * vecs[0:1, :] + vecs[1:2, :]).astype(BF16)
    proj[...] = nn(normed, w_qkv[...]) + bias_qkv[...]
    cos = take_rows(cosine[...], start)
    sin = take_rows(sine[...], start)
    for t in range(TILES):
        lanes = slice(t * LANES, (t + 1) * LANES)
        q = proj[:, t * LANES : (t + 1) * LANES] * SCALE
        q_out[0, t] = (q * cos + rolled(q) * sin).astype(BF16)
        k = proj[:, D + t * LANES : D + (t + 1) * LANES]
        k_out[0, t] = (k * cos + rolled(k) * sin).astype(BF16)
        v_out[0, t] = proj[:, 2 * D + t * LANES : 2 * D + (t + 1) * LANES].astype(BF16)

    key_lanes = key_side(length)
    ones = jnp.ones((L, LANES), BF16)
    query_lanes = jnp.where(lane_iota(LANES, LANES) % HW == 3, 1.0, 0.0).astype(BF16)
    head = lane_iota(LANES, LANES) // HW

    def tile(t, carry):
        for h, part in enumerate(stack_heads(jnp.concatenate([k_out[0, t], key_lanes], axis=1))):
            keys_big[h * L : (h + 1) * L, :] = part
        for h, part in enumerate(stack_heads(jnp.concatenate([v_out[0, t], ones], axis=1))):
            values_big[h * L : (h + 1) * L, :] = part
        for block in range(L // LANES):
            part = slice(block * LANES, (block + 1) * LANES)
            queries = jnp.concatenate([q_out[0, t, part, :], query_lanes], axis=1)
            raised = []
            tops = jnp.zeros((LANES, LANES), F32)
            for h in range(GROUP):
                scores = nt(queries, keys_big[h * L : (h + 1) * L, :])
                top = jnp.max(scores, axis=1, keepdims=True)
                raised.append(jnp.exp(scores - top).astype(BF16))
                tops = jnp.where(head == h, top, tops)
            sums = nn(jnp.concatenate(raised, axis=1), values_big[...])
            total = sums[:, LANES:]
            mixed_out[0, t, part, :] = (sums[:, :LANES] / total).astype(BF16)
            lse_out[0, t, part, :] = split_lanes(-(tops + jnp.log(total)), 1.0)
        return carry

    lax.fori_loop(0, TILES, tile, 0)


def middle_kernel(
    rows,
    lengths, x_in, mixed_in, cotangent, packed_hbm, vecs, bias_up,
    act_out, grad_mid_out, grad_mixed_out, dots_out,
    g_packed, g_vecs, g_bias_up, stats,
    w_out, w_up, w_down, a_out, a_up, a_down, staging, arrived,
):
    window = pl.program_id(0)
    packed = g_packed

    @pl.when(window == 0)
    def _():
        for ref in (a_out, a_up, a_down, g_vecs, g_bias_up, stats):
            ref[...] = jnp.zeros_like(ref)
        fetch = pltpu.make_async_copy(packed_hbm, packed, arrived)
        fetch.start()
        fetch.wait()
        if rows:
            steps = FF // D

            def copy_down(i, carry):
                at = pl.multiple_of(i * steps * rows, steps * rows)
                w_down[pl.ds(at, steps * rows), :] = packed[i, : steps * rows, :]
                return carry

            lax.fori_loop(0, D // rows, copy_down, 0)
            parts = [(packed, (steps + c) * rows, c * D, D) for c in range(steps)]
            unpack_rows(parts, rows, staging, w_up)
            unpack_rows([(packed, 2 * steps * rows, 0, D)], rows, staging, w_out)
        else:
            w_down[...] = packed[:FF, :]
            for c in range(FF // D):
                w_up[:, c * D : (c + 1) * D] = packed[FF + c * D : FF + (c + 1) * D, :]
            w_out[...] = packed[2 * FF :, :]

    count = x_in.shape[0]
    height = count * L
    x = x_in[...].reshape(height, D).astype(F32)
    mixed = jnp.concatenate(
        [
            jnp.concatenate([mixed_in[w, t] for t in range(TILES)], axis=1)
            for w in range(count)
        ],
        axis=0,
    )
    attn = nn(mixed, w_out[...]) + vecs[2:3, :]
    middle = x + attn
    n, inverse = normalize(middle)
    normed = (n * vecs[0:1, :] + vecs[1:2, :]).astype(BF16)
    row = lax.broadcasted_iota(jnp.int32, (L, 1), 0)
    valid = jnp.concatenate(
        [jnp.where(row < lengths[window * count + w], 1.0, 0.0) for w in range(count)], axis=0
    )
    grad_result = cotangent[...].reshape(height, D).astype(F32) * valid
    grad_ffn = grad_result.astype(BF16)
    ffn = jnp.zeros((height, D), F32)
    grad_normed = jnp.zeros((height, D), F32)
    for c in range(FF // CHUNK):
        cols = slice(c * CHUNK, (c + 1) * CHUNK)
        up = w_up[:, cols]
        down = w_down[cols, :]
        pre = nn(normed, up) + bias_up[:, cols]
        phi = 0.5 + 0.5 * lax.erf(pre * math.sqrt(0.5))
        hidden = (pre * phi).astype(BF16)
        slope = phi + pre * (jnp.exp(-0.5 * pre * pre) * (1.0 / math.sqrt(2.0 * math.pi)))
        ffn = ffn + nn(hidden, down)
        grad_pre = (nt(grad_ffn, down) * slope).astype(BF16)
        a_up[:, cols] += tn(normed, grad_pre)
        a_down[cols, :] += tn(hidden, grad_ffn)
        g_bias_up[:, cols] += col_sum(grad_pre.astype(F32))
        grad_normed = grad_normed + nt(grad_pre, up)
    ffn = ffn + vecs[3:4, :]
    result = middle + ffn
    act_out[...] = result.astype(BF16).reshape(count, L, D)
    stats[0:1, :] += col_sum(valid * result * result)
    stats[1:2, :] += col_sum(valid * attn * attn)
    stats[2:3, :] += col_sum(valid * ffn * ffn)
    grad_middle = grad_result + norm_back(grad_normed * vecs[0:1, :], n, inverse)
    grad_mid_out[...] = grad_middle.reshape(count, L, D)
    grad_attn = grad_middle.astype(BF16)
    a_out[...] += tn(mixed, grad_attn)
    g_vecs[0:1, :] += col_sum(grad_normed * n)
    g_vecs[1:2, :] += col_sum(grad_normed)
    g_vecs[2:3, :] += col_sum(grad_attn.astype(F32))
    g_vecs[3:4, :] += col_sum(grad_ffn.astype(F32))
    grad_mixed = nt(grad_attn, w_out[...]).astype(BF16)
    first = lax.broadcasted_iota(jnp.int32, (LANES, LANES), 0) // HW
    same = jnp.where(first == lane_iota(LANES, LANES) // HW, 1.0, 0.0).astype(BF16)
    for t in range(TILES):
        lanes = slice(t * LANES, (t + 1) * LANES)
        part = grad_mixed[:, lanes]
        product = part.astype(F32) * mixed[:, lanes].astype(F32)
        high = product.astype(BF16)
        low = (product - high.astype(F32)).astype(BF16)
        dots = split_lanes(-(nn(high, same) + nn(low, same)), 0.0)
        for w in range(count):
            grad_mixed_out[w, t] = part[w * L : (w + 1) * L]
            dots_out[w, t] = dots[w * L : (w + 1) * L]

    @pl.when(window == pl.num_programs(0) - 1)
    def _():
        steps = FF // D
        if rows:
            parts = [((steps + c) * rows, a_up, c * D) for c in range(steps)]
            parts.append((2 * steps * rows, a_out, 0))

            def group(i, carry):
                at = pl.multiple_of(i * 2 * rows, 2 * rows)
                for first, ref, col in parts:
                    block = ref[pl.ds(at, 2 * rows), col : col + D]
                    staging[first : first + rows, :D] = block[:rows]
                    staging[first : first + rows, D : 2 * D] = block[rows:]
                for j in range(2):
                    top = pl.multiple_of((2 * i + j) * steps * rows, steps * rows)
                    g_packed[2 * i + j, : steps * rows, :] = a_down[
                        pl.ds(top, steps * rows), :
                    ].astype(BF16)
                    g_packed[2 * i + j, steps * rows :, :] = staging[
                        steps * rows : g_packed.shape[1], j * D : (j + 1) * D
                    ].astype(BF16)
                return carry

            lax.fori_loop(0, D // (2 * rows), group, 0)
        else:
            g_packed[:FF, :] = a_down[...].astype(BF16)
            for c in range(steps):
                g_packed[FF + c * D : FF + (c + 1) * D, :] = a_up[
                    :, c * D : (c + 1) * D
                ].astype(BF16)
            g_packed[2 * FF :, :] = a_out[...].astype(BF16)


def back_kernel(
    rows,
    offsets, lengths, x_in, q_in, k_in, v_in, lse_in, gm_in, dots_in, grad_mid, w_qkv, vecs,
    cosine, sine,
    span_grad, g_first, g_second, g_vecs, g_bias,
    a_qkv, grad_proj, queries_big, mixed_big, scores_back,
):
    window = pl.program_id(0)
    start = offsets[window]
    length = lengths[window]

    @pl.when(window == 0)
    def _():
        for ref in (a_qkv, g_vecs, g_bias):
            ref[...] = jnp.zeros_like(ref)

    cos = take_rows(cosine[...], start)
    sin = take_rows(sine[...], start)
    key_lanes = key_side(length)
    at = lane_iota(L, LANES) % HW
    value_lanes = jnp.where(at < 3, 1.0, 0.0).astype(BF16)
    for t in range(TILES):
        queries = jnp.concatenate([q_in[0, t], lse_in[0, t]], axis=1)
        for h, part in enumerate(stack_heads(queries)):
            queries_big[h * L : (h + 1) * L, :] = part
        mixed = jnp.concatenate([gm_in[0, t], dots_in[0, t]], axis=1)
        for h, part in enumerate(stack_heads(mixed)):
            mixed_big[h * L : (h + 1) * L, :] = part
        keys = jnp.concatenate([k_in[0, t], key_lanes], axis=1)
        values = jnp.concatenate([v_in[0, t], value_lanes], axis=1)
        for block in range(L // LANES):
            here = slice(block * LANES, (block + 1) * LANES)
            low_probs = []
            for h in range(GROUP):
                heads = slice(h * L, (h + 1) * L)
                probs = jnp.exp(nt(keys[here, :], queries_big[heads, :]))
                back = probs * nt(values[here, :], mixed_big[heads, :])
                scores_back[here, h * L : (h + 1) * L] = back.astype(BF16)
                low_probs.append(probs.astype(BF16))
            grad_v = nn(jnp.concatenate(low_probs, axis=1), mixed_big[:, :LANES])
            grad_k = nn(scores_back[here, :], queries_big[:, :LANES])
            grad_k = grad_k * cos[here, :] - rolled(grad_k) * sin[here, :]
            grad_proj[here, D + t * LANES : D + (t + 1) * LANES] = grad_k.astype(BF16)
            grad_proj[here, 2 * D + t * LANES : 2 * D + (t + 1) * LANES] = grad_v.astype(BF16)
        turned = nn(k_in[0, t].T, scores_back[...])
        grad_q = jnp.concatenate(
            [turned[h * HW : (h + 1) * HW, h * L : (h + 1) * L] for h in range(GROUP)], axis=0
        ).T
        grad_q = (grad_q * cos - rolled(grad_q) * sin) * SCALE
        grad_proj[:, t * LANES : (t + 1) * LANES] = grad_q.astype(BF16)
    x = x_in[0].astype(F32)
    n, inverse = normalize(x)
    normed = (n * vecs[0:1, :] + vecs[1:2, :]).astype(BF16)
    grads = grad_proj[...]
    a_qkv[...] += tn(normed, grads)
    g_bias[...] += col_sum(grads.astype(F32))
    grad_normed = nt(grads, w_qkv[...])
    g_vecs[0:1, :] += col_sum(grad_normed * n)
    g_vecs[1:2, :] += col_sum(grad_normed)
    grad_x = grad_mid[0] + norm_back(grad_normed * vecs[0:1, :], n, inverse)
    wide = jnp.concatenate([grad_x, jnp.zeros((CROP, D), F32)], axis=0)
    span_grad[0] = pltpu.roll(wide, start, 0).astype(BF16)

    @pl.when(window == pl.num_programs(0) - 1)
    def _():
        cut = g_first.shape[-1]
        if rows:

            def group(i, carry):
                at = pl.multiple_of(i * 2 * rows, 2 * rows)
                block = a_qkv[pl.ds(at, 2 * rows), :]
                for j in range(2):
                    part = block[j * rows : (j + 1) * rows].astype(BF16)
                    g_first[2 * i + j] = part[:, :cut]
                    g_second[2 * i + j] = part[:, cut:]
                return carry

            lax.fori_loop(0, D // (2 * rows), group, 0)
        else:
            g_first[...] = a_qkv[:, :cut].astype(BF16)
            g_second[...] = a_qkv[:, cut:].astype(BF16)


def rows_spec(*dims, count=1):
    rank = len(dims)
    return pl.BlockSpec((count,) + dims, lambda w, *_: (w,) + (0,) * rank)


def whole_spec(*dims):
    rank = len(dims)
    return pl.BlockSpec(dims, lambda w, *_: (0,) * rank, pipeline_mode=pl.Buffered(1))


def call(kernel, scalars, windows, in_specs, outs, scratch, name):
    return pl.pallas_call(
        kernel,
        out_shape=[jax.ShapeDtypeStruct(shape, dtype) for _, shape, dtype in outs],
        grid_spec=pltpu.PrefetchScalarGridSpec(
            num_scalar_prefetch=scalars,
            grid=(windows,),
            in_specs=in_specs,
            out_specs=[spec for spec, _, _ in outs],
            scratch_shapes=scratch,
        ),
        compiler_params=pltpu.CompilerParams(
            dimension_semantics=("arbitrary",), vmem_limit_bytes=63 * 1024 * 1024
        ),
        name=name,
    )


def flat_index():
    return lax.axis_index("wa") * lax.axis_size("an") + lax.axis_index("an")


def swap(value, bit, devices):
    return lax.ppermute(value, BOTH, [(i, i ^ (1 << bit)) for i in range(devices)])


def gather_steps(shards, orders, devices):
    index = flat_index()
    done = [[] for _ in shards]
    values = list(shards)
    for step in range(len(orders[0])):
        for i, order in enumerate(orders):
            bit = order[step]
            mine = values[i]
            other = swap(mine, bit, devices)
            low = ((index >> bit) & 1) == 0
            axis = sum(1 for b in done[i] if b > bit)
            values[i] = jnp.stack(
                [jnp.where(low, mine, other), jnp.where(low, other, mine)], axis=axis
            )
            done[i].append(bit)
    return [v.reshape((devices,) + s.shape) for v, s in zip(values, shards)]


def scatter_steps(arrays, orders, devices):
    index = flat_index()
    bits = devices.bit_length() - 1
    left = [sorted(range(bits), reverse=True) for _ in arrays]
    values = [a.reshape((2,) * bits + a.shape[1:]) for a in arrays]
    for step in range(bits):
        for i, order in enumerate(orders):
            bit = order[step]
            axis = left[i].index(bit)
            own = (index >> bit) & 1
            send = lax.dynamic_index_in_dim(values[i], 1 - own, axis, keepdims=False)
            keep = lax.dynamic_index_in_dim(values[i], own, axis, keepdims=False)
            got = swap(send.astype(BF16), bit, devices)
            values[i] = keep.astype(F32) + got.astype(F32)
            left[i].remove(bit)
    return values


def rotary_tables():
    inverse = 10000.0 ** (-jnp.arange(0, HW, 2, dtype=F32) / HW)
    angles = jnp.arange(SPAN, dtype=jnp.int32).astype(F32)[:, None] * inverse
    cosine = jnp.tile(jnp.cos(angles), (1, 2 * GROUP))
    sine = jnp.sin(angles)
    sine = jnp.tile(jnp.concatenate([-sine, sine], axis=1), (1, GROUP))
    return cosine, sine


def body(
    span_states,
    offsets,
    lengths,
    cotangent,
    qkv_weight,
    out_weight,
    up_weight,
    down_weight,
    up_bias,
    norm_gains,
    norm_shifts,
    qkv_bias,
    out_biases,
):
    windows = span_states.shape[0]
    wa, an = lax.axis_size("wa"), lax.axis_size("an")
    devices = wa * an
    bits = devices.bit_length() - 1
    steps = FF // D
    rows = D // devices if D % (4 * devices) == 0 and devices == 1 << bits else 0
    cut = 8 * LANES
    small = jnp.concatenate([norm_gains, norm_shifts, qkv_bias, out_biases], axis=0)
    if rows:
        down_order = list(range(bits))[::-1]
        other_order = list(down_order)
        other_order[-2], other_order[-3] = other_order[-3], other_order[-2]
        shard = qkv_weight.reshape(rows, 3 * D)
        extra = jnp.concatenate([small.reshape(-1), up_bias])
        extra = jnp.pad(extra, (0, cut - extra.shape[0]))[None]
        w_first, w_second = gather_steps(
            [jnp.concatenate([shard[:, :cut], extra], axis=0), shard[:, cut:]],
            [down_order, other_order],
            devices,
        )
        extra = w_first[:, rows]
        share = D // wa
        small = extra[::an, : 9 * share].reshape(wa, 9, share).transpose(1, 0, 2)
        small = small.reshape(9, D).astype(F32)
        up_share = FF // devices
        extra = extra[:, 9 * share : 9 * share + up_share]
        bias_up = extra.astype(F32).reshape(1, FF)
        up = up_weight.reshape(rows, steps, D).transpose(1, 0, 2).reshape(steps * rows, D)
        pack_rows = -(-(2 * steps + 1) * rows // 32) * 32
        pad = jnp.zeros((pack_rows - (2 * steps + 1) * rows, D), BF16)
        packed = jnp.concatenate([down_weight.reshape(-1, D), up, out_weight.reshape(-1, D), pad])
        packed = lax.all_gather(packed, BOTH, axis=0, tiled=False)
    else:
        w_qkv = lax.all_gather(qkv_weight, BOTH, axis=0, tiled=True).reshape(D, 3 * D)
        w_first, w_second = w_qkv[:, :cut], w_qkv[:, cut:]
        small = lax.all_gather(small, "wa", axis=1, tiled=True).astype(F32)
        bias_up = lax.all_gather(up_bias, BOTH, axis=0, tiled=True).astype(F32).reshape(1, FF)
        w_down = lax.all_gather(down_weight, BOTH, axis=0, tiled=True).reshape(FF, D)
        w_up = lax.all_gather(up_weight, BOTH, axis=0, tiled=True)
        w_up = w_up.reshape(D, steps, D).transpose(1, 0, 2).reshape(FF, D)
        w_out = lax.all_gather(out_weight, BOTH, axis=0, tiled=True).reshape(D, D)
        packed = jnp.concatenate([w_down, w_up, w_out], axis=0)
    vec_one = jnp.stack([small[0], small[2]])
    vec_two = jnp.stack([small[1], small[3], small[7], small[8]])
    bias_qkv = small[4:7].reshape(1, 3 * D)
    cosine, sine = rotary_tables()

    tiled_spec = rows_spec(TILES, L, LANES)
    tiled_shape = (windows, TILES, L, LANES)
    flat_spec = rows_spec(L, D)
    flat_shape = (windows, L, D)
    pair = 2 if windows % 2 == 0 else 1
    tiled_pair = rows_spec(TILES, L, LANES, count=pair)
    flat_pair = rows_spec(L, D, count=pair)
    table_spec = whole_spec(SPAN, LANES)

    tiled_out = (tiled_spec, tiled_shape, BF16)

    def kept(shape, dtype):
        return (whole_spec(*shape), shape, dtype)

    x, q, k, v, lse, mixed, w_qkv = call(
        functools.partial(front_kernel, rows),
        2,
        windows,
        [
            rows_spec(SPAN, D),
            whole_spec(*w_first.shape),
            whole_spec(*w_second.shape),
            whole_spec(2, D),
            whole_spec(1, 3 * D),
            table_spec,
            table_spec,
        ],
        [(flat_spec, flat_shape, BF16)] + [tiled_out] * 5 + [kept((D, 3 * D), BF16)],
        [
            pltpu.VMEM((L, 3 * D), F32),
            pltpu.VMEM((GROUP * L, 2 * LANES), BF16),
            pltpu.VMEM((GROUP * L, 2 * LANES), BF16),
            pltpu.VMEM((max(4 * rows, 8), 3 * D), F32),
        ],
        "front",
    )(offsets, lengths, span_states, w_first, w_second, vec_one, bias_qkv, cosine, sine)

    activations, grad_mid, grad_mixed, dots, g_packed, g_vec_two, g_bias_up, stats = call(
        functools.partial(middle_kernel, rows),
        1,
        windows // pair,
        [
            flat_pair,
            tiled_pair,
            flat_pair,
            pl.BlockSpec(memory_space=pl.ANY),
            whole_spec(4, D),
            whole_spec(1, FF),
        ],
        [
            (flat_pair, flat_shape, BF16),
            (flat_pair, flat_shape, F32),
            (tiled_pair, tiled_shape, BF16),
            (tiled_pair, tiled_shape, BF16),
            kept(packed.shape, BF16),
            kept((4, D), F32),
            kept((1, FF), F32),
            kept((3, D), F32),
        ],
        [
            pltpu.VMEM((D, D), BF16),
            pltpu.VMEM((D, FF), BF16),
            pltpu.VMEM((FF, D), BF16),
            pltpu.VMEM((D, D), F32),
            pltpu.VMEM((D, FF), F32),
            pltpu.VMEM((FF, D), F32),
            pltpu.VMEM((packed.shape[1] if rows else 8, FF), F32),
            pltpu.SemaphoreType.DMA(()),
        ],
        "middle",
    )(lengths, x, mixed, cotangent, packed, vec_two, bias_up)

    if rows:
        packed_shard = lax.psum_scatter(g_packed, BOTH, scatter_dimension=0, tiled=False)
        packed_shard = packed_shard.astype(F32)
        down_grad = packed_shard[: steps * rows].reshape(-1)
        up_grad = packed_shard[steps * rows : 2 * steps * rows].reshape(steps, rows, D)
        up_grad = up_grad.transpose(1, 0, 2).reshape(-1)
        out_grad = packed_shard[2 * steps * rows : (2 * steps + 1) * rows].reshape(-1)
    else:

        def scatter_flat(grad):
            flat = grad.reshape(devices, -1)
            return lax.psum_scatter(flat, BOTH, scatter_dimension=0, tiled=False).astype(F32)

        down_grad = scatter_flat(g_packed[:FF])
        g_up = g_packed[FF : 2 * FF].reshape(steps, D, D).transpose(1, 0, 2)
        up_grad = scatter_flat(g_up)
        out_grad = scatter_flat(g_packed[2 * FF :])

    span_grad, g_first, g_second, g_vec_one, g_bias_qkv = call(
        functools.partial(back_kernel, rows),
        2,
        windows,
        [flat_spec]
        + [tiled_spec] * 6
        + [flat_spec, whole_spec(D, 3 * D), whole_spec(2, D), table_spec, table_spec],
        [
            (rows_spec(SPAN, D), (windows, SPAN, D), BF16),
            kept((devices, rows, cut) if rows else w_first.shape, BF16),
            kept(w_second.shape, BF16),
            kept((2, D), F32),
            kept((1, 3 * D), F32),
        ],
        [
            pltpu.VMEM((D, 3 * D), F32),
            pltpu.VMEM((L, 3 * D), BF16),
            pltpu.VMEM((GROUP * L, 2 * LANES), BF16),
            pltpu.VMEM((GROUP * L, 2 * LANES), BF16),
            pltpu.VMEM((L, GROUP * L), BF16),
        ],
        "back",
    )(offsets, lengths, x, q, k, v, lse, grad_mixed, dots, grad_mid, w_qkv, vec_one, cosine, sine)

    token_count = jnp.sum(lengths).astype(F32)
    totals = jnp.concatenate([jnp.sum(stats, axis=1), token_count[None]])
    vec_sums = jnp.concatenate([g_vec_one, g_vec_two, g_bias_qkv.reshape(3, D)], axis=0)
    share = D // wa
    up_share = FF // devices
    if rows:
        vec_sums = vec_sums.reshape(9, wa, share).transpose(1, 0, 2).reshape(wa, 1, 9 * share)
        vec_sums = jnp.broadcast_to(vec_sums, (wa, an, 9 * share)).reshape(devices, 9 * share)
        ride = jnp.concatenate(
            [
                vec_sums,
                g_bias_up.reshape(devices, up_share),
                jnp.broadcast_to(totals, (devices, 4)),
                jnp.zeros((devices, cut - 9 * share - up_share - 4), F32),
            ],
            axis=1,
        )
        g_first = jnp.concatenate([g_first, ride.astype(BF16)[:, None]], axis=1)
        g_first, g_second = scatter_steps(
            [g_first, g_second], [down_order[::-1], other_order[::-1]], devices
        )
        qkv_grad = jnp.concatenate([g_first[:rows], g_second], axis=1).reshape(-1)
        ride = g_first[rows]
        shares = ride[: 9 * share].reshape(9, share)
        up_bias_grad = ride[9 * share : 9 * share + up_share]
        totals = ride[9 * share + up_share : 9 * share + up_share + 4]
    else:
        qkv_grad = scatter_flat(jnp.concatenate([g_first, g_second], axis=1))
        vec_sums, up_sums, totals = lax.psum((vec_sums, g_bias_up.reshape(FF), totals), BOTH)
        shares = lax.dynamic_slice_in_dim(vec_sums, lax.axis_index("wa") * share, share, 1)
        up_bias_grad = lax.dynamic_slice_in_dim(up_sums, flat_index() * up_share, up_share, 0)
    root_means = jnp.sqrt(totals[:3] / (totals[3] * D))
    return (
        activations,
        span_grad,
        qkv_grad,
        out_grad,
        up_grad,
        down_grad,
        up_bias_grad,
        jnp.stack([shares[0], shares[2]]),
        jnp.stack([shares[1], shares[3]]),
        shares[6:9],
        shares[4:6],
        root_means,
    )


def solution(mesh):
    return jax.shard_map(
        body,
        mesh=mesh,
        in_specs=(
            P(("wa", "an"), None, None),
            P(("wa", "an")),
            P(("wa", "an")),
            P(("wa", "an"), None, None),
            P(("wa", "an")),
            P(("wa", "an")),
            P(("wa", "an")),
            P(("wa", "an")),
            P(("wa", "an")),
            P(None, "wa"),
            P(None, "wa"),
            P(None, "wa"),
            P(None, "wa"),
        ),
        out_specs=(
            P(("wa", "an"), None, None),
            P(("wa", "an"), None, None),
            P(("wa", "an")),
            P(("wa", "an")),
            P(("wa", "an")),
            P(("wa", "an")),
            P(("wa", "an")),
            P(None, "wa"),
            P(None, "wa"),
            P(None, "wa"),
            P(None, "wa"),
            P(),
        ),
        check_vma=False,
    )
```

```python
import functools
import math

import jax
import jax.numpy as jnp
from jax import lax
from jax.experimental import pallas as pl
from jax.experimental.pallas import tpu as pltpu
from jax.sharding import PartitionSpec as P

D = 640
HEADS = 20
FF = 2560
L = 384
CROP = 128
SPAN = L + CROP
HW = D // HEADS
LANES = 128
TILES = D // LANES
GROUP = LANES // HW
SCALE = HW**-0.5
CHUNK = 512
F32 = jnp.float32
BF16 = jnp.bfloat16
BOTH = ("wa", "an")


def nn(a, b):
    return lax.dot_general(a, b, (((1,), (0,)), ((), ())), preferred_element_type=F32)


def nt(a, b):
    return lax.dot_general(a, b, (((1,), (1,)), ((), ())), preferred_element_type=F32)


def tn(a, b):
    return lax.dot_general(a, b, (((0,), (0,)), ((), ())), preferred_element_type=F32)


def lane_iota(rows, cols):
    return lax.broadcasted_iota(jnp.int32, (rows, cols), 1)


def normalize(v):
    centred = v - jnp.mean(v, axis=-1, keepdims=True)
    inverse = lax.rsqrt(jnp.mean(centred * centred, axis=-1, keepdims=True) + 1e-05)
    return centred * inverse, inverse


def norm_back(d, n, inverse):
    return inverse * (
        d - jnp.mean(d, axis=-1, keepdims=True) - n * jnp.mean(d * n, axis=-1, keepdims=True)
    )


def col_sum(v):
    return jnp.sum(v, axis=0, keepdims=True)


def split_lanes(v, last):
    high = v.astype(BF16).astype(F32)
    rest = v - high
    mid = rest.astype(BF16).astype(F32)
    low = rest - mid
    at = lane_iota(*v.shape) % HW
    out = jnp.where(at == 0, high, jnp.where(at == 1, mid, jnp.where(at == 2, low, 0.0)))
    return jnp.where(at == 3, last, out).astype(BF16)


def rolled(v):
    first = (lane_iota(*v.shape) % HW) < HW // 2
    ahead = pltpu.roll(v, LANES - HW // 2, 1)
    behind = pltpu.roll(v, HW // 2, 1)
    return jnp.where(first, ahead, behind)


def stack_heads(wide):
    head = (lane_iota(1, 2 * LANES) % LANES) // HW
    return [jnp.where(head == h, wide, jnp.zeros_like(wide)) for h in range(GROUP)]


def key_side(length):
    at = lane_iota(L, LANES) % HW
    row = lax.broadcasted_iota(jnp.int32, (L, LANES), 0)
    bias = jnp.where(row < length, 0.0, -1e30)
    return jnp.where(at < 3, 1.0, jnp.where(at == 3, bias, 0.0)).astype(BF16)


def take_rows(full, start):
    return pltpu.roll(full, (SPAN - start) % SPAN, 0)[:L]


def unpack_rows(parts, rows, staging, dest):
    def group(i, carry):
        for ref, first, col, cols in parts:
            for j in range(4):
                low = first // 16 * 16
                high = min(-(-(first + rows) // 16) * 16, ref.shape[1])
                block = ref[4 * i + j, low:high, :].astype(F32)
                staging[j * rows : (j + 1) * rows, col : col + cols] = block[
                    first - low : first - low + rows
                ]
        at = pl.multiple_of(i * 4 * rows, 4 * rows)
        dest[pl.ds(at, 4 * rows), :] = staging[: 4 * rows, : dest.shape[1]].astype(BF16)
        return carry

    lax.fori_loop(0, dest.shape[0] // (4 * rows), group, 0)


def unpack_cores(parts, mine, rows, staging, dest):
    def group(i, carry):
        for own, other, col, cols in parts:
            for j in range(4):
                at = 2 * i + j // 2
                block = jnp.where(
                    mine == j % 2, own[at].astype(F32)[:rows], other[at].astype(F32)[:rows]
                )
                staging[j * rows : (j + 1) * rows, col : col + cols] = block
        at = pl.multiple_of(i * 4 * rows, 4 * rows)
        dest[pl.ds(at, 4 * rows), :] = staging[...].astype(BF16)
        return carry

    lax.fori_loop(0, dest.shape[0] // (4 * rows), group, 0)


def front_kernel(
    rows,
    offsets, lengths, core, span, *refs,
):
    (
        weights, small, cosine, sine,
        x_out, q_out, k_out, v_out, lse_out, mixed_out, w_qkv,
        proj, keys_big, values_big, staging,
    ) = refs[:-14], *refs[-14:]
    window = pl.program_id(0)

    @pl.when(window == 0)
    def _():
        if rows:
            own_first, other_first, own_second, other_second = weights
            cut = own_first.shape[2]
            parts = [
                (own_first, other_first, 0, cut),
                (own_second, other_second, cut, 3 * D - cut),
            ]
            unpack_cores(parts, core[0], rows, staging, w_qkv)
        else:
            w_qkv[...] = weights[0][...]

    start = offsets[window]
    length = lengths[window]
    x = take_rows(span[0].astype(F32), start)
    x_out[0] = x.astype(BF16)
    n, _ = normalize(x)
    normed = (n * small[0:1, :] + small[2:3, :]).astype(BF16)
    bias = jnp.concatenate([small[4:5, :], small[5:6, :], small[6:7, :]], axis=1)
    proj[...] = nn(normed, w_qkv[...]) + bias
    cos = take_rows(cosine[...], start)
    sin = take_rows(sine[...], start)
    for t in range(TILES):
        lanes = slice(t * LANES, (t + 1) * LANES)
        q = proj[:, t * LANES : (t + 1) * LANES] * SCALE
        q_out[0, t] = (q * cos + rolled(q) * sin).astype(BF16)
        k = proj[:, D + t * LANES : D + (t + 1) * LANES]
        k_out[0, t] = (k * cos + rolled(k) * sin).astype(BF16)
        v_out[0, t] = proj[:, 2 * D + t * LANES : 2 * D + (t + 1) * LANES].astype(BF16)

    key_lanes = key_side(length)
    ones = jnp.ones((L, LANES), BF16)
    query_lanes = jnp.where(lane_iota(LANES, LANES) % HW == 3, 1.0, 0.0).astype(BF16)
    head = lane_iota(LANES, LANES) // HW

    def tile(t, carry):
        for h, part in enumerate(stack_heads(jnp.concatenate([k_out[0, t], key_lanes], axis=1))):
            keys_big[h * L : (h + 1) * L, :] = part
        for h, part in enumerate(stack_heads(jnp.concatenate([v_out[0, t], ones], axis=1))):
            values_big[h * L : (h + 1) * L, :] = part
        for block in range(L // LANES):
            part = slice(block * LANES, (block + 1) * LANES)
            queries = jnp.concatenate([q_out[0, t, part, :], query_lanes], axis=1)
            raised = []
            tops = jnp.zeros((LANES, LANES), F32)
            for h in range(GROUP):
                scores = nt(queries, keys_big[h * L : (h + 1) * L, :])
                top = jnp.max(scores, axis=1, keepdims=True)
                raised.append(jnp.exp(scores - top).astype(BF16))
                tops = jnp.where(head == h, top, tops)
            sums = nn(jnp.concatenate(raised, axis=1), values_big[...])
            total = sums[:, LANES:]
            mixed_out[0, t, part, :] = (sums[:, :LANES] / total).astype(BF16)
            lse_out[0, t, part, :] = split_lanes(-(tops + jnp.log(total)), 1.0)
        return carry

    lax.fori_loop(0, TILES, tile, 0)


def middle_kernel(
    rows,
    lengths, x_in, mixed_in, cotangent, packed_hbm, small, bias_up,
    act_out, grad_mid_out, grad_mixed_out, dots_out,
    g_packed, g_vecs, g_bias_up, stats,
    w_out, w_up, w_down, a_out, a_up, a_down, staging, arrived,
):
    window = pl.program_id(0)
    packed = g_packed

    @pl.when(window == 0)
    def _():
        for ref in (a_out, a_up, a_down, g_vecs, g_bias_up, stats):
            ref[...] = jnp.zeros_like(ref)
        fetch = pltpu.make_async_copy(packed_hbm, packed, arrived)
        fetch.start()
        fetch.wait()
        if rows:
            steps = FF // D

            def copy_down(i, carry):
                at = pl.multiple_of(i * steps * rows, steps * rows)
                w_down[pl.ds(at, steps * rows), :] = packed[i, : steps * rows, :]
                return carry

            lax.fori_loop(0, D // rows, copy_down, 0)
            parts = [(packed, (steps + c) * rows, c * D, D) for c in range(steps)]
            unpack_rows(parts, rows, staging, w_up)
            unpack_rows([(packed, 2 * steps * rows, 0, D)], rows, staging, w_out)
        else:
            w_down[...] = packed[:FF, :]
            for c in range(FF // D):
                w_up[:, c * D : (c + 1) * D] = packed[FF + c * D : FF + (c + 1) * D, :]
            w_out[...] = packed[2 * FF :, :]

    count = x_in.shape[0]
    height = count * L
    x = x_in[...].reshape(height, D).astype(F32)
    mixed = jnp.concatenate(
        [
            jnp.concatenate([mixed_in[w, t] for t in range(TILES)], axis=1)
            for w in range(count)
        ],
        axis=0,
    )
    attn = nn(mixed, w_out[...]) + small[7:8, :]
    middle = x + attn
    n, inverse = normalize(middle)
    normed = (n * small[1:2, :] + small[3:4, :]).astype(BF16)
    row = lax.broadcasted_iota(jnp.int32, (L, 1), 0)
    valid = jnp.concatenate(
        [jnp.where(row < lengths[window * count + w], 1.0, 0.0) for w in range(count)], axis=0
    )
    grad_result = cotangent[...].reshape(height, D).astype(F32) * valid
    grad_ffn = grad_result.astype(BF16)
    ffn = jnp.zeros((height, D), F32)
    grad_normed = jnp.zeros((height, D), F32)
    for c in range(FF // CHUNK):
        cols = slice(c * CHUNK, (c + 1) * CHUNK)
        up = w_up[:, cols]
        down = w_down[cols, :]
        pre = nn(normed, up) + bias_up[:, cols]
        phi = 0.5 + 0.5 * lax.erf(pre * math.sqrt(0.5))
        hidden = (pre * phi).astype(BF16)
        slope = phi + pre * (jnp.exp(-0.5 * pre * pre) * (1.0 / math.sqrt(2.0 * math.pi)))
        ffn = ffn + nn(hidden, down)
        grad_pre = (nt(grad_ffn, down) * slope).astype(BF16)
        a_up[:, cols] += tn(normed, grad_pre)
        a_down[cols, :] += tn(hidden, grad_ffn)
        g_bias_up[:, cols] += col_sum(grad_pre.astype(F32))
        grad_normed = grad_normed + nt(grad_pre, up)
    ffn = ffn + small[8:9, :]
    result = middle + ffn
    act_out[...] = result.astype(BF16).reshape(count, L, D)
    stats[0:1, :] += col_sum(valid * result * result)
    stats[1:2, :] += col_sum(valid * attn * attn)
    stats[2:3, :] += col_sum(valid * ffn * ffn)
    grad_middle = grad_result + norm_back(grad_normed * small[1:2, :], n, inverse)
    grad_mid_out[...] = grad_middle.reshape(count, L, D)
    grad_attn = grad_middle.astype(BF16)
    a_out[...] += tn(mixed, grad_attn)
    g_vecs[0:1, :] += col_sum(grad_normed * n)
    g_vecs[1:2, :] += col_sum(grad_normed)
    g_vecs[2:3, :] += col_sum(grad_attn.astype(F32))
    g_vecs[3:4, :] += col_sum(grad_ffn.astype(F32))
    grad_mixed = nt(grad_attn, w_out[...]).astype(BF16)
    first = lax.broadcasted_iota(jnp.int32, (LANES, LANES), 0) // HW
    same = jnp.where(first == lane_iota(LANES, LANES) // HW, 1.0, 0.0).astype(BF16)
    for t in range(TILES):
        lanes = slice(t * LANES, (t + 1) * LANES)
        part = grad_mixed[:, lanes]
        product = part.astype(F32) * mixed[:, lanes].astype(F32)
        high = product.astype(BF16)
        low = (product - high.astype(F32)).astype(BF16)
        dots = split_lanes(-(nn(high, same) + nn(low, same)), 0.0)
        for w in range(count):
            grad_mixed_out[w, t] = part[w * L : (w + 1) * L]
            dots_out[w, t] = dots[w * L : (w + 1) * L]

    @pl.when(window == pl.num_programs(0) - 1)
    def _():
        steps = FF // D
        if rows:
            parts = [((steps + c) * rows, a_up, c * D) for c in range(steps)]
            parts.append((2 * steps * rows, a_out, 0))

            def group(i, carry):
                at = pl.multiple_of(i * 2 * rows, 2 * rows)
                for first, ref, col in parts:
                    block = ref[pl.ds(at, 2 * rows), col : col + D]
                    staging[first : first + rows, :D] = block[:rows]
                    staging[first : first + rows, D : 2 * D] = block[rows:]
                for j in range(2):
                    top = pl.multiple_of((2 * i + j) * steps * rows, steps * rows)
                    g_packed[2 * i + j, : steps * rows, :] = a_down[
                        pl.ds(top, steps * rows), :
                    ].astype(BF16)
                    g_packed[2 * i + j, steps * rows :, :] = staging[
                        steps * rows : g_packed.shape[1], j * D : (j + 1) * D
                    ].astype(BF16)
                return carry

            lax.fori_loop(0, D // (2 * rows), group, 0)
        else:
            g_packed[:FF, :] = a_down[...].astype(BF16)
            for c in range(steps):
                g_packed[FF + c * D : FF + (c + 1) * D, :] = a_up[
                    :, c * D : (c + 1) * D
                ].astype(BF16)
            g_packed[2 * FF :, :] = a_out[...].astype(BF16)


def back_kernel(
    rows, inner,
    offsets, lengths, core, x_in, q_in, k_in, v_in, lse_in, gm_in, dots_in, grad_mid, w_qkv, small,
    cosine, sine, vec_two, bias_up, stats,
    span_grad, keep_first, send_first, keep_second, send_second, g_vecs, g_bias,
    a_qkv, grad_proj, queries_big, mixed_big, scores_back, ride, staging,
):
    window = pl.program_id(0)
    start = offsets[window]
    length = lengths[window]

    @pl.when(window == 0)
    def _():
        for ref in (a_qkv, g_vecs, g_bias):
            ref[...] = jnp.zeros_like(ref)

    cos = take_rows(cosine[...], start)
    sin = take_rows(sine[...], start)
    key_lanes = key_side(length)
    at = lane_iota(L, LANES) % HW
    value_lanes = jnp.where(at < 3, 1.0, 0.0).astype(BF16)
    for t in range(TILES):
        queries = jnp.concatenate([q_in[0, t], lse_in[0, t]], axis=1)
        for h, part in enumerate(stack_heads(queries)):
            queries_big[h * L : (h + 1) * L, :] = part
        mixed = jnp.concatenate([gm_in[0, t], dots_in[0, t]], axis=1)
        for h, part in enumerate(stack_heads(mixed)):
            mixed_big[h * L : (h + 1) * L, :] = part
        keys = jnp.concatenate([k_in[0, t], key_lanes], axis=1)
        values = jnp.concatenate([v_in[0, t], value_lanes], axis=1)
        for block in range(L // LANES):
            here = slice(block * LANES, (block + 1) * LANES)
            low_probs = []
            for h in range(GROUP):
                heads = slice(h * L, (h + 1) * L)
                probs = jnp.exp(nt(keys[here, :], queries_big[heads, :]))
                back = probs * nt(values[here, :], mixed_big[heads, :])
                scores_back[here, h * L : (h + 1) * L] = back.astype(BF16)
                low_probs.append(probs.astype(BF16))
            grad_v = nn(jnp.concatenate(low_probs, axis=1), mixed_big[:, :LANES])
            grad_k = nn(scores_back[here, :], queries_big[:, :LANES])
            grad_k = grad_k * cos[here, :] - rolled(grad_k) * sin[here, :]
            grad_proj[here, D + t * LANES : D + (t + 1) * LANES] = grad_k.astype(BF16)
            grad_proj[here, 2 * D + t * LANES : 2 * D + (t + 1) * LANES] = grad_v.astype(BF16)
        turned = nn(k_in[0, t].T, scores_back[...])
        grad_q = jnp.concatenate(
            [turned[h * HW : (h + 1) * HW, h * L : (h + 1) * L] for h in range(GROUP)], axis=0
        ).T
        grad_q = (grad_q * cos - rolled(grad_q) * sin) * SCALE
        grad_proj[:, t * LANES : (t + 1) * LANES] = grad_q.astype(BF16)
    x = x_in[0].astype(F32)
    n, inverse = normalize(x)
    normed = (n * small[0:1, :] + small[2:3, :]).astype(BF16)
    grads = grad_proj[...]
    a_qkv[...] += tn(normed, grads)
    g_bias[...] += col_sum(grads.astype(F32))
    grad_normed = nt(grads, w_qkv[...])
    g_vecs[0:1, :] += col_sum(grad_normed * n)
    g_vecs[1:2, :] += col_sum(grad_normed)
    grad_x = grad_mid[0] + norm_back(grad_normed * small[0:1, :], n, inverse)
    wide = jnp.concatenate([grad_x, jnp.zeros((CROP, D), F32)], axis=0)
    span_grad[0] = pltpu.roll(wide, start, 0).astype(BF16)

    @pl.when(window == pl.num_programs(0) - 1)
    def _():
        if not rows:
            keep_first[...] = a_qkv[...].astype(BF16)
            for ref in (send_first, keep_second, send_second):
                ref[...] = jnp.zeros_like(ref)
            return
        cut = keep_first.shape[2]
        groups, _, share = bias_up.shape
        ride[...] = jnp.zeros_like(ride)
        staging[...] = jnp.zeros_like(staging)
        bias = g_bias[...]
        vectors = jnp.concatenate(
            [g_vecs[...], vec_two[...]] + [bias[:, i * D : (i + 1) * D] for i in range(3)], axis=0
        )
        parts = ride.shape[0]
        width = D // parts
        for w in range(parts):
            ride[w, 0:9, 0:width] = vectors[:, w * width : (w + 1) * width]
        sums = jnp.sum(stats[...], axis=1, keepdims=True)
        tokens = lax.fori_loop(
            0, pl.num_programs(0), lambda w, total: total + lengths[w], jnp.int32(0)
        ).astype(F32)
        at = lane_iota(1, LANES)
        last = jnp.where(at == 3, tokens, 0.0)
        for i in range(3):
            last = jnp.where(at == i, sums[i : i + 1, :], last)
        mine = core[0]

        def group(i, carry):
            at = pl.multiple_of(i * 2 * rows, 2 * rows)
            block = a_qkv[pl.ds(at, 2 * rows), :]
            low, high = block[:rows], block[rows:]
            vecs = ride[2 * i // inner]
            for j, first, second in ((0, keep_first, keep_second), (1, send_first, send_second)):
                want = mine == j
                staging[:rows, :] = jnp.where(want, low, high)
                staging[rows : rows + 4, :LANES] = vecs[0:4]
                staging[rows : rows + 4, LANES : 2 * LANES] = vecs[4:8]
                staging[rows : rows + 1, 2 * LANES : 3 * LANES] = vecs[8:9]
                staging[rows + 1 : rows + 2, 2 * LANES : 2 * LANES + share] = jnp.where(
                    want, bias_up[2 * i], bias_up[2 * i + 1]
                )
                staging[rows + 2 : rows + 3, 2 * LANES : 3 * LANES] = last
                first[i] = staging[:, :cut].astype(BF16)
                second[i] = staging[:rows, cut:].astype(BF16)
            return carry

        lax.fori_loop(0, groups // 2, group, 0)


def rows_spec(*dims, count=1):
    rank = len(dims)
    return pl.BlockSpec((count,) + dims, lambda w, *_: (w,) + (0,) * rank)


def whole_spec(*dims):
    rank = len(dims)
    return pl.BlockSpec(dims, lambda w, *_: (0,) * rank, pipeline_mode=pl.Buffered(1))


def call(kernel, scalars, windows, in_specs, outs, scratch, name):
    return pl.pallas_call(
        kernel,
        out_shape=[jax.ShapeDtypeStruct(shape, dtype) for _, shape, dtype in outs],
        grid_spec=pltpu.PrefetchScalarGridSpec(
            num_scalar_prefetch=scalars,
            grid=(windows,),
            in_specs=in_specs,
            out_specs=[spec for spec, _, _ in outs],
            scratch_shapes=scratch,
        ),
        compiler_params=pltpu.CompilerParams(
            dimension_semantics=("arbitrary",), vmem_limit_bytes=63 * 1024 * 1024
        ),
        name=name,
    )


def flat_index():
    return lax.axis_index("wa") * lax.axis_size("an") + lax.axis_index("an")


def swap(value, bit, devices):
    return lax.ppermute(value, BOTH, [(i, i ^ (1 << bit)) for i in range(devices)])


def gather_steps(shards, orders, devices):
    index = flat_index()
    done = [[] for _ in shards]
    values = list(shards)
    for step in range(len(orders[0]) - 1):
        for i, order in enumerate(orders):
            bit = order[step]
            mine = values[i]
            other = swap(mine, bit, devices)
            low = ((index >> bit) & 1) == 0
            axis = sum(1 for b in done[i] if b > bit)
            values[i] = jnp.stack(
                [jnp.where(low, mine, other), jnp.where(low, other, mine)], axis=axis
            )
            done[i].append(bit)
    values = [v.reshape((devices // 2,) + s.shape) for v, s in zip(values, shards)]
    return [(v, swap(v, 0, devices)) for v in values]


def scatter_steps(halves, orders, devices):
    index = flat_index()
    bits = devices.bit_length() - 1
    left = [list(range(bits - 1, 0, -1)) for _ in halves]
    shape = (2,) * (bits - 1)
    values = []
    for keep, send in halves:
        got = swap(send, 0, devices)
        values.append((keep.reshape(shape + keep.shape[1:]), got.reshape(shape + keep.shape[1:])))
    for step in range(1, bits):
        for i, order in enumerate(orders):
            bit = order[step]
            axis = left[i].index(bit)
            own = (index >> bit) & 1

            def half(which):
                keep, got = (
                    lax.dynamic_index_in_dim(v, which, axis, keepdims=False).astype(F32)
                    for v in values[i]
                )
                return keep + got

            got = swap(half(1 - own).astype(BF16), bit, devices)
            values[i] = (half(own), got)
            left[i].remove(bit)
    return [keep + got.astype(F32) for keep, got in values]


def rotary_tables():
    inverse = 10000.0 ** (-jnp.arange(0, HW, 2, dtype=F32) / HW)
    angles = jnp.arange(SPAN, dtype=jnp.int32).astype(F32)[:, None] * inverse
    cosine = jnp.tile(jnp.cos(angles), (1, 2 * GROUP))
    sine = jnp.sin(angles)
    sine = jnp.tile(jnp.concatenate([-sine, sine], axis=1), (1, GROUP))
    return cosine, sine


def body(
    span_states,
    offsets,
    lengths,
    cotangent,
    qkv_weight,
    out_weight,
    up_weight,
    down_weight,
    up_bias,
    norm_gains,
    norm_shifts,
    qkv_bias,
    out_biases,
):
    windows = span_states.shape[0]
    wa, an = lax.axis_size("wa"), lax.axis_size("an")
    devices = wa * an
    bits = devices.bit_length() - 1
    steps = FF // D
    even = D % (4 * devices) == 0 and devices == 1 << bits and an % 2 == 0
    rows = D // devices if even else 0
    cut = 8 * LANES
    share = D // wa
    up_share = FF // devices
    core = (flat_index() & 1).astype(jnp.int32)[None]
    small = jnp.concatenate([norm_gains, norm_shifts, qkv_bias, out_biases], axis=0)
    if rows:
        down_order = list(range(bits))[::-1]
        other_order = list(down_order)
        other_order[-2], other_order[-3] = other_order[-3], other_order[-2]
        shard = qkv_weight.reshape(rows, 3 * D)
        extra = jnp.concatenate([small.reshape(-1), up_bias])
        extra = jnp.pad(extra, (0, cut - extra.shape[0]))[None]
        (own_first, other_first), (own_second, other_second) = gather_steps(
            [jnp.concatenate([shard[:, :cut], extra], axis=0), shard[:, cut:]],
            [down_order, other_order],
            devices,
        )
        weights = [own_first, other_first, own_second, other_second]
        small = own_first[:: an // 2, rows, : 9 * share]
        small = small.reshape(wa, 9, share).transpose(1, 0, 2).reshape(9, D).astype(F32)
        ups = [v[:, rows, 9 * share : 9 * share + up_share] for v in (own_first, other_first)]
        low = core[0] == 0
        bias_up = jnp.stack(
            [jnp.where(low, ups[0], ups[1]), jnp.where(low, ups[1], ups[0])], axis=1
        )
        bias_up = bias_up.astype(F32).reshape(1, FF)
        up = up_weight.reshape(rows, steps, D).transpose(1, 0, 2).reshape(steps * rows, D)
        pack_rows = -(-(2 * steps + 1) * rows // 32) * 32
        pad = jnp.zeros((pack_rows - (2 * steps + 1) * rows, D), BF16)
        packed = jnp.concatenate([down_weight.reshape(-1, D), up, out_weight.reshape(-1, D), pad])
        packed = lax.all_gather(packed, BOTH, axis=0, tiled=False)
    else:
        w_qkv = lax.all_gather(qkv_weight, BOTH, axis=0, tiled=True).reshape(D, 3 * D)
        weights = [w_qkv]
        small = lax.all_gather(small, "wa", axis=1, tiled=True).astype(F32)
        bias_up = lax.all_gather(up_bias, BOTH, axis=0, tiled=True).astype(F32).reshape(1, FF)
        w_down = lax.all_gather(down_weight, BOTH, axis=0, tiled=True).reshape(FF, D)
        w_up = lax.all_gather(up_weight, BOTH, axis=0, tiled=True)
        w_up = w_up.reshape(D, steps, D).transpose(1, 0, 2).reshape(FF, D)
        w_out = lax.all_gather(out_weight, BOTH, axis=0, tiled=True).reshape(D, D)
        packed = jnp.concatenate([w_down, w_up, w_out], axis=0)
    cosine, sine = rotary_tables()

    tiled_spec = rows_spec(TILES, L, LANES)
    tiled_shape = (windows, TILES, L, LANES)
    flat_spec = rows_spec(L, D)
    flat_shape = (windows, L, D)
    pair = 1
    tiled_pair = rows_spec(TILES, L, LANES, count=pair)
    flat_pair = rows_spec(L, D, count=pair)
    table_spec = whole_spec(SPAN, LANES)

    tiled_out = (tiled_spec, tiled_shape, BF16)

    def kept(shape, dtype):
        return (whole_spec(*shape), shape, dtype)

    x, q, k, v, lse, mixed, w_qkv = call(
        functools.partial(front_kernel, rows),
        3,
        windows,
        [rows_spec(SPAN, D)]
        + [whole_spec(*w.shape) for w in weights]
        + [whole_spec(9, D), table_spec, table_spec],
        [(flat_spec, flat_shape, BF16)] + [tiled_out] * 5 + [kept((D, 3 * D), BF16)],
        [
            pltpu.VMEM((L, 3 * D), F32),
            pltpu.VMEM((GROUP * L, 2 * LANES), BF16),
            pltpu.VMEM((GROUP * L, 2 * LANES), BF16),
            pltpu.VMEM((max(4 * rows, 8), 3 * D), F32),
        ],
        "front",
    )(offsets, lengths, core, span_states, *weights, small, cosine, sine)

    activations, grad_mid, grad_mixed, dots, g_packed, g_vec_two, g_bias_up, stats = call(
        functools.partial(middle_kernel, rows),
        1,
        windows // pair,
        [
            flat_pair,
            tiled_pair,
            flat_pair,
            pl.BlockSpec(memory_space=pl.ANY),
            whole_spec(9, D),
            whole_spec(1, FF),
        ],
        [
            (flat_pair, flat_shape, BF16),
            (flat_pair, flat_shape, F32),
            (tiled_pair, tiled_shape, BF16),
            (tiled_pair, tiled_shape, BF16),
            kept(packed.shape, BF16),
            kept((4, D), F32),
            kept((1, FF), F32),
            kept((3, D), F32),
        ],
        [
            pltpu.VMEM((D, D), BF16),
            pltpu.VMEM((D, FF), BF16),
            pltpu.VMEM((FF, D), BF16),
            pltpu.VMEM((D, D), F32),
            pltpu.VMEM((D, FF), F32),
            pltpu.VMEM((FF, D), F32),
            pltpu.VMEM((packed.shape[1] if rows else 8, FF), F32),
            pltpu.SemaphoreType.DMA(()),
        ],
        "middle",
    )(lengths, x, mixed, cotangent, packed, small, bias_up)

    if rows:
        packed_shard = lax.psum_scatter(g_packed, BOTH, scatter_dimension=0, tiled=False)
        packed_shard = packed_shard.astype(F32)
        down_grad = packed_shard[: steps * rows].reshape(-1)
        up_grad = packed_shard[steps * rows : 2 * steps * rows].reshape(steps, rows, D)
        up_grad = up_grad.transpose(1, 0, 2).reshape(-1)
        out_grad = packed_shard[2 * steps * rows : (2 * steps + 1) * rows].reshape(-1)
    else:

        def scatter_flat(grad):
            flat = grad.reshape(devices, -1)
            return lax.psum_scatter(flat, BOTH, scatter_dimension=0, tiled=False).astype(F32)

        down_grad = scatter_flat(g_packed[:FF])
        g_up = g_packed[FF : 2 * FF].reshape(steps, D, D).transpose(1, 0, 2)
        up_grad = scatter_flat(g_up)
        out_grad = scatter_flat(g_packed[2 * FF :])

    half = devices // 2
    if rows:
        shape_first, shape_second = (half, rows + 4, cut), (half, rows, 3 * D - cut)
        halves = [shape_first, shape_first, shape_second, shape_second]
        bias_up_rows = g_bias_up.reshape(devices, 1, up_share)
    else:
        halves = [(D, 3 * D)] + [(8, LANES)] * 3
        bias_up_rows = jnp.zeros((devices, 1, up_share), F32)
    span_grad, *halves, g_vec_one, g_bias_qkv = call(
        functools.partial(back_kernel, rows, an),
        3,
        windows,
        [flat_spec]
        + [tiled_spec] * 6
        + [flat_spec, whole_spec(D, 3 * D), whole_spec(9, D), table_spec, table_spec]
        + [whole_spec(4, D), whole_spec(devices, 1, up_share), whole_spec(3, D)],
        [(rows_spec(SPAN, D), (windows, SPAN, D), BF16)]
        + [kept(shape, BF16) for shape in halves]
        + [kept((2, D), F32), kept((1, 3 * D), F32)],
        [
            pltpu.VMEM((D, 3 * D), F32),
            pltpu.VMEM((L, 3 * D), BF16),
            pltpu.VMEM((GROUP * L, 2 * LANES), BF16),
            pltpu.VMEM((GROUP * L, 2 * LANES), BF16),
            pltpu.VMEM((L, GROUP * L), BF16),
            pltpu.VMEM((wa if rows else 1, 16, LANES), F32),
            pltpu.VMEM((rows + 4, 3 * D), F32),
        ],
        "back",
    )(
        offsets, lengths, core, x, q, k, v, lse, grad_mixed, dots, grad_mid, w_qkv, small,
        cosine, sine, g_vec_two, bias_up_rows, stats,
    )

    if rows:
        g_first, g_second = scatter_steps(
            [halves[:2], halves[2:]], [down_order[::-1], other_order[::-1]], devices
        )
        qkv_grad = jnp.concatenate([g_first[:rows], g_second], axis=1).reshape(-1)
        ride = g_first[rows:]
        third = ride[:, 2 * LANES : 3 * LANES]
        shares = jnp.concatenate(
            [ride[:, :share], ride[:, LANES : LANES + share], third[:1, :share]], axis=0
        )
        up_bias_grad = third[1, :up_share]
        totals = third[2, :4]
    else:
        qkv_grad = scatter_flat(halves[0])
        token_count = jnp.sum(lengths).astype(F32)
        totals = jnp.concatenate([jnp.sum(stats, axis=1), token_count[None]])
        vec_sums = jnp.concatenate([g_vec_one, g_vec_two, g_bias_qkv.reshape(3, D)], axis=0)
        vec_sums, up_sums, totals = lax.psum((vec_sums, g_bias_up.reshape(FF), totals), BOTH)
        shares = lax.dynamic_slice_in_dim(vec_sums, lax.axis_index("wa") * share, share, 1)
        up_bias_grad = lax.dynamic_slice_in_dim(up_sums, flat_index() * up_share, up_share, 0)
    root_means = jnp.sqrt(totals[:3] / (totals[3] * D))
    return (
        activations,
        span_grad,
        qkv_grad,
        out_grad,
        up_grad,
        down_grad,
        up_bias_grad,
        jnp.stack([shares[0], shares[2]]),
        jnp.stack([shares[1], shares[3]]),
        shares[6:9],
        shares[4:6],
        root_means,
    )


def solution(mesh):
    return jax.shard_map(
        body,
        mesh=mesh,
        in_specs=(
            P(("wa", "an"), None, None),
            P(("wa", "an")),
            P(("wa", "an")),
            P(("wa", "an"), None, None),
            P(("wa", "an")),
            P(("wa", "an")),
            P(("wa", "an")),
            P(("wa", "an")),
            P(("wa", "an")),
            P(None, "wa"),
            P(None, "wa"),
            P(None, "wa"),
            P(None, "wa"),
        ),
        out_specs=(
            P(("wa", "an"), None, None),
            P(("wa", "an"), None, None),
            P(("wa", "an")),
            P(("wa", "an")),
            P(("wa", "an")),
            P(("wa", "an")),
            P(("wa", "an")),
            P(None, "wa"),
            P(None, "wa"),
            P(None, "wa"),
            P(None, "wa"),
            P(),
        ),
        check_vma=False,
    )
```

```python
import functools
import math

import jax
import jax.numpy as jnp
import numpy as np
from jax import lax
from jax.experimental import pallas as pl
from jax.experimental.pallas import tpu as pltpu
from jax.sharding import PartitionSpec as P

D = 640
HEADS = 20
FF = 2560
L = 384
CROP = 128
SPAN = L + CROP
HW = D // HEADS
LANES = 128
TILES = D // LANES
GROUP = LANES // HW
SCALE = HW**-0.5
CHUNK = 512
F32 = jnp.float32
BF16 = jnp.bfloat16
BOTH = ("wa", "an")


def nn(a, b):
    return lax.dot_general(a, b, (((1,), (0,)), ((), ())), preferred_element_type=F32)


def nt(a, b):
    return lax.dot_general(a, b, (((1,), (1,)), ((), ())), preferred_element_type=F32)


def tn(a, b):
    return lax.dot_general(a, b, (((0,), (0,)), ((), ())), preferred_element_type=F32)


def lane_iota(rows, cols):
    return lax.broadcasted_iota(jnp.int32, (rows, cols), 1)


def normalize(v):
    centred = v - jnp.mean(v, axis=-1, keepdims=True)
    inverse = lax.rsqrt(jnp.mean(centred * centred, axis=-1, keepdims=True) + 1e-05)
    return centred * inverse, inverse


def norm_back(d, n, inverse):
    return inverse * (
        d - jnp.mean(d, axis=-1, keepdims=True) - n * jnp.mean(d * n, axis=-1, keepdims=True)
    )


def col_sum(v):
    return jnp.sum(v, axis=0, keepdims=True)


def split_lanes(v, last):
    high = v.astype(BF16).astype(F32)
    rest = v - high
    mid = rest.astype(BF16).astype(F32)
    low = rest - mid
    at = lane_iota(*v.shape) % HW
    out = jnp.where(at == 0, high, jnp.where(at == 1, mid, jnp.where(at == 2, low, 0.0)))
    return jnp.where(at == 3, last, out).astype(BF16)


def rolled(v):
    first = (lane_iota(*v.shape) % HW) < HW // 2
    ahead = pltpu.roll(v, LANES - HW // 2, 1)
    behind = pltpu.roll(v, HW // 2, 1)
    return jnp.where(first, ahead, behind)


def stack_heads(wide):
    head = (lane_iota(1, 2 * LANES) % LANES) // HW
    return [jnp.where(head == h, wide, jnp.zeros_like(wide)) for h in range(GROUP)]


def key_side(length):
    at = lane_iota(L, LANES) % HW
    row = lax.broadcasted_iota(jnp.int32, (L, LANES), 0)
    bias = jnp.where(row < length, 0.0, -1e30)
    return jnp.where(at < 3, 1.0, jnp.where(at == 3, bias, 0.0)).astype(BF16)


def picks(rows, cols, shift):
    row = lax.broadcasted_iota(jnp.int32, (rows, cols), 0)
    return jnp.where(lane_iota(rows, cols) - row == shift, 1.0, 0.0).astype(BF16)


def turn_tables(cosine, sine, offset):
    cos_off, sin_off = offset[0, 0:1, :], offset[0, 1:2, :]
    cos, sin = cosine[...], sine[...]
    return cos * cos_off - sin * sin_off, sin * cos_off + cos * sin_off


def unpack_rows(parts, rows, staging, dest):
    def group(i, carry):
        for ref, first, col, cols in parts:
            for j in range(4):
                low = first // 16 * 16
                high = min(-(-(first + rows) // 16) * 16, ref.shape[1])
                block = ref[4 * i + j, low:high, :].astype(F32)
                staging[j * rows : (j + 1) * rows, col : col + cols] = block[
                    first - low : first - low + rows
                ]
        at = pl.multiple_of(i * 4 * rows, 4 * rows)
        dest[pl.ds(at, 4 * rows), :] = staging[: 4 * rows, : dest.shape[1]].astype(BF16)
        return carry

    lax.fori_loop(0, dest.shape[0] // (4 * rows), group, 0)


def unpack_cores(parts, mine, rows, staging, dest):
    def group(i, carry):
        for own, other, col, cols in parts:
            for j in range(4):
                at = 2 * i + j // 2
                block = jnp.where(
                    mine == j % 2, own[at].astype(F32)[:rows], other[at].astype(F32)[:rows]
                )
                staging[j * rows : (j + 1) * rows, col : col + cols] = block
        at = pl.multiple_of(i * 4 * rows, 4 * rows)
        dest[pl.ds(at, 4 * rows), :] = staging[...].astype(BF16)
        return carry

    lax.fori_loop(0, dest.shape[0] // (4 * rows), group, 0)


def front_kernel(
    rows,
    offsets, lengths, core, span, *refs,
):
    (
        weights, small, cosine, sine, offset,
        x_out, q_out, k_out, v_out, lse_out, mixed_out, w_qkv,
        proj, keys_big, values_big, staging,
    ) = refs[:-15], *refs[-15:]
    window = pl.program_id(0)

    @pl.when(window == 0)
    def _():
        if rows:
            own_first, other_first, own_second, other_second = weights
            cut = own_first.shape[2]
            parts = [
                (own_first, other_first, 0, cut),
                (own_second, other_second, cut, 3 * D - cut),
            ]
            unpack_cores(parts, core[0], rows, staging, w_qkv)
        else:
            w_qkv[...] = weights[0][...]

    start = offsets[window]
    length = lengths[window]
    x = nn(picks(L, SPAN, start), span[0])
    x_out[0] = x.astype(BF16)
    n, _ = normalize(x)
    normed = (n * small[0:1, :] + small[2:3, :]).astype(BF16)
    bias = jnp.concatenate([small[4:5, :], small[5:6, :], small[6:7, :]], axis=1)
    proj[...] = nn(normed, w_qkv[...]) + bias
    cos, sin = turn_tables(cosine, sine, offset)
    for t in range(TILES):
        lanes = slice(t * LANES, (t + 1) * LANES)
        q = proj[:, t * LANES : (t + 1) * LANES] * SCALE
        q_out[0, t] = (q * cos + rolled(q) * sin).astype(BF16)
        k = proj[:, D + t * LANES : D + (t + 1) * LANES]
        k_out[0, t] = (k * cos + rolled(k) * sin).astype(BF16)
        v_out[0, t] = proj[:, 2 * D + t * LANES : 2 * D + (t + 1) * LANES].astype(BF16)

    key_lanes = key_side(length)
    ones = jnp.ones((L, LANES), BF16)
    query_lanes = jnp.where(lane_iota(LANES, LANES) % HW == 3, 1.0, 0.0).astype(BF16)
    head = lane_iota(LANES, LANES) // HW

    def tile(t, carry):
        for h, part in enumerate(stack_heads(jnp.concatenate([k_out[0, t], key_lanes], axis=1))):
            keys_big[h * L : (h + 1) * L, :] = part
        for h, part in enumerate(stack_heads(jnp.concatenate([v_out[0, t], ones], axis=1))):
            values_big[h * L : (h + 1) * L, :] = part
        for block in range(L // LANES):
            part = slice(block * LANES, (block + 1) * LANES)
            queries = jnp.concatenate([q_out[0, t, part, :], query_lanes], axis=1)
            raised = []
            tops = jnp.zeros((LANES, LANES), F32)
            for h in range(GROUP):
                scores = nt(queries, keys_big[h * L : (h + 1) * L, :])
                top = jnp.max(scores, axis=1, keepdims=True)
                raised.append(jnp.exp(scores - top).astype(BF16))
                tops = jnp.where(head == h, top, tops)
            sums = nn(jnp.concatenate(raised, axis=1), values_big[...])
            total = sums[:, LANES:]
            mixed_out[0, t, part, :] = (sums[:, :LANES] / total).astype(BF16)
            lse_out[0, t, part, :] = split_lanes(-(tops + jnp.log(total)), 1.0)
        return carry

    lax.fori_loop(0, TILES, tile, 0)


def middle_kernel(
    rows,
    lengths, x_in, mixed_in, cotangent, packed_hbm, small, bias_up,
    act_out, grad_mid_out, grad_mixed_out, dots_out,
    g_packed, g_vecs, g_bias_up, stats,
    w_out, w_up, w_down, a_out, a_up, a_down, staging, arrived,
):
    window = pl.program_id(0)
    packed = g_packed

    @pl.when(window == 0)
    def _():
        for ref in (a_out, a_up, a_down, g_vecs, g_bias_up, stats):
            ref[...] = jnp.zeros_like(ref)
        fetch = pltpu.make_async_copy(packed_hbm, packed, arrived)
        fetch.start()
        fetch.wait()
        if rows:
            steps = FF // D

            def copy_down(i, carry):
                at = pl.multiple_of(i * steps * rows, steps * rows)
                w_down[pl.ds(at, steps * rows), :] = packed[i, : steps * rows, :]
                return carry

            lax.fori_loop(0, D // rows, copy_down, 0)
            parts = [(packed, (steps + c) * rows, c * D, D) for c in range(steps)]
            unpack_rows(parts, rows, staging, w_up)
            unpack_rows([(packed, 2 * steps * rows, 0, D)], rows, staging, w_out)
        else:
            w_down[...] = packed[:FF, :]
            for c in range(FF // D):
                w_up[:, c * D : (c + 1) * D] = packed[FF + c * D : FF + (c + 1) * D, :]
            w_out[...] = packed[2 * FF :, :]

    count = x_in.shape[0]
    height = count * L
    x = x_in[...].reshape(height, D).astype(F32)
    mixed = jnp.concatenate(
        [
            jnp.concatenate([mixed_in[w, t] for t in range(TILES)], axis=1)
            for w in range(count)
        ],
        axis=0,
    )
    attn = nn(mixed, w_out[...]) + small[7:8, :]
    middle = x + attn
    n, inverse = normalize(middle)
    normed = (n * small[1:2, :] + small[3:4, :]).astype(BF16)
    row = lax.broadcasted_iota(jnp.int32, (L, 1), 0)
    valid = jnp.concatenate(
        [jnp.where(row < lengths[window * count + w], 1.0, 0.0) for w in range(count)], axis=0
    )
    grad_result = cotangent[...].reshape(height, D).astype(F32) * valid
    grad_ffn = grad_result.astype(BF16)
    ffn = jnp.zeros((height, D), F32)
    grad_normed = jnp.zeros((height, D), F32)
    for c in range(FF // CHUNK):
        cols = slice(c * CHUNK, (c + 1) * CHUNK)
        up = w_up[:, cols]
        down = w_down[cols, :]
        pre = nn(normed, up) + bias_up[:, cols]
        phi = 0.5 + 0.5 * lax.erf(pre * math.sqrt(0.5))
        hidden = (pre * phi).astype(BF16)
        slope = phi + pre * (jnp.exp(-0.5 * pre * pre) * (1.0 / math.sqrt(2.0 * math.pi)))
        ffn = ffn + nn(hidden, down)
        grad_pre = (nt(grad_ffn, down) * slope).astype(BF16)
        a_up[:, cols] += tn(normed, grad_pre)
        a_down[cols, :] += tn(hidden, grad_ffn)
        g_bias_up[:, cols] += col_sum(grad_pre.astype(F32))
        grad_normed = grad_normed + nt(grad_pre, up)
    ffn = ffn + small[8:9, :]
    result = middle + ffn
    act_out[...] = result.astype(BF16).reshape(count, L, D)
    stats[0:1, :] += col_sum(valid * result * result)
    stats[1:2, :] += col_sum(valid * attn * attn)
    stats[2:3, :] += col_sum(valid * ffn * ffn)
    grad_middle = grad_result + norm_back(grad_normed * small[1:2, :], n, inverse)
    grad_mid_out[...] = grad_middle.reshape(count, L, D)
    grad_attn = grad_middle.astype(BF16)
    a_out[...] += tn(mixed, grad_attn)
    g_vecs[0:1, :] += col_sum(grad_normed * n)
    g_vecs[1:2, :] += col_sum(grad_normed)
    g_vecs[2:3, :] += col_sum(grad_attn.astype(F32))
    g_vecs[3:4, :] += col_sum(grad_ffn.astype(F32))
    grad_mixed = nt(grad_attn, w_out[...]).astype(BF16)
    first = lax.broadcasted_iota(jnp.int32, (LANES, LANES), 0) // HW
    same = jnp.where(first == lane_iota(LANES, LANES) // HW, 1.0, 0.0).astype(BF16)
    for t in range(TILES):
        lanes = slice(t * LANES, (t + 1) * LANES)
        part = grad_mixed[:, lanes]
        product = part.astype(F32) * mixed[:, lanes].astype(F32)
        high = product.astype(BF16)
        low = (product - high.astype(F32)).astype(BF16)
        dots = split_lanes(-(nn(high, same) + nn(low, same)), 0.0)
        for w in range(count):
            grad_mixed_out[w, t] = part[w * L : (w + 1) * L]
            dots_out[w, t] = dots[w * L : (w + 1) * L]

    @pl.when(window == pl.num_programs(0) - 1)
    def _():
        steps = FF // D
        if rows:
            parts = [((steps + c) * rows, a_up, c * D) for c in range(steps)]
            parts.append((2 * steps * rows, a_out, 0))

            def group(i, carry):
                at = pl.multiple_of(i * 2 * rows, 2 * rows)
                for first, ref, col in parts:
                    block = ref[pl.ds(at, 2 * rows), col : col + D]
                    staging[first : first + rows, :D] = block[:rows]
                    staging[first : first + rows, D : 2 * D] = block[rows:]
                for j in range(2):
                    top = pl.multiple_of((2 * i + j) * steps * rows, steps * rows)
                    g_packed[2 * i + j, : steps * rows, :] = a_down[
                        pl.ds(top, steps * rows), :
                    ].astype(BF16)
                    g_packed[2 * i + j, steps * rows :, :] = staging[
                        steps * rows : g_packed.shape[1], j * D : (j + 1) * D
                    ].astype(BF16)
                return carry

            lax.fori_loop(0, D // (2 * rows), group, 0)
        else:
            g_packed[:FF, :] = a_down[...].astype(BF16)
            for c in range(steps):
                g_packed[FF + c * D : FF + (c + 1) * D, :] = a_up[
                    :, c * D : (c + 1) * D
                ].astype(BF16)
            g_packed[2 * FF :, :] = a_out[...].astype(BF16)


def back_kernel(
    rows, inner,
    offsets, lengths, core, x_in, q_in, k_in, v_in, lse_in, gm_in, dots_in, grad_mid, w_qkv, small,
    cosine, sine, offset, vec_two, bias_up, stats,
    span_grad, keep_first, send_first, keep_second, send_second, g_vecs, g_bias,
    a_qkv, grad_proj, queries_big, mixed_big, scores_back, ride, staging,
):
    window = pl.program_id(0)
    start = offsets[window]
    length = lengths[window]

    @pl.when(window == 0)
    def _():
        for ref in (a_qkv, g_vecs, g_bias):
            ref[...] = jnp.zeros_like(ref)

    cos, sin = turn_tables(cosine, sine, offset)
    key_lanes = key_side(length)
    at = lane_iota(L, LANES) % HW
    value_lanes = jnp.where(at < 3, 1.0, 0.0).astype(BF16)
    for t in range(TILES):
        queries = jnp.concatenate([q_in[0, t], lse_in[0, t]], axis=1)
        for h, part in enumerate(stack_heads(queries)):
            queries_big[h * L : (h + 1) * L, :] = part
        mixed = jnp.concatenate([gm_in[0, t], dots_in[0, t]], axis=1)
        for h, part in enumerate(stack_heads(mixed)):
            mixed_big[h * L : (h + 1) * L, :] = part
        keys = jnp.concatenate([k_in[0, t], key_lanes], axis=1)
        values = jnp.concatenate([v_in[0, t], value_lanes], axis=1)
        for block in range(L // LANES):
            here = slice(block * LANES, (block + 1) * LANES)
            low_probs = []
            for h in range(GROUP):
                heads = slice(h * L, (h + 1) * L)
                probs = jnp.exp(nt(keys[here, :], queries_big[heads, :]))
                back = probs * nt(values[here, :], mixed_big[heads, :])
                scores_back[here, h * L : (h + 1) * L] = back.astype(BF16)
                low_probs.append(probs.astype(BF16))
            grad_v = nn(jnp.concatenate(low_probs, axis=1), mixed_big[:, :LANES])
            grad_k = nn(scores_back[here, :], queries_big[:, :LANES])
            grad_k = grad_k * cos[here, :] - rolled(grad_k) * sin[here, :]
            grad_proj[here, D + t * LANES : D + (t + 1) * LANES] = grad_k.astype(BF16)
            grad_proj[here, 2 * D + t * LANES : 2 * D + (t + 1) * LANES] = grad_v.astype(BF16)
        turned = nn(k_in[0, t].T, scores_back[...])
        grad_q = jnp.concatenate(
            [turned[h * HW : (h + 1) * HW, h * L : (h + 1) * L] for h in range(GROUP)], axis=0
        ).T
        grad_q = (grad_q * cos - rolled(grad_q) * sin) * SCALE
        grad_proj[:, t * LANES : (t + 1) * LANES] = grad_q.astype(BF16)
    x = x_in[0].astype(F32)
    n, inverse = normalize(x)
    normed = (n * small[0:1, :] + small[2:3, :]).astype(BF16)
    grads = grad_proj[...]
    a_qkv[...] += tn(normed, grads)
    g_bias[...] += col_sum(grads.astype(F32))
    grad_normed = nt(grads, w_qkv[...])
    g_vecs[0:1, :] += col_sum(grad_normed * n)
    g_vecs[1:2, :] += col_sum(grad_normed)
    grad_x = grad_mid[0] + norm_back(grad_normed * small[0:1, :], n, inverse)
    wide = jnp.concatenate([grad_x, jnp.zeros((CROP, D), F32)], axis=0)
    span_grad[0] = pltpu.roll(wide, start, 0).astype(BF16)

    @pl.when(window == pl.num_programs(0) - 1)
    def _():
        if not rows:
            keep_first[...] = a_qkv[...].astype(BF16)
            for ref in (send_first, keep_second, send_second):
                ref[...] = jnp.zeros_like(ref)
            return
        cut = keep_first.shape[2]
        groups, _, share = bias_up.shape
        ride[...] = jnp.zeros_like(ride)
        staging[...] = jnp.zeros_like(staging)
        bias = g_bias[...]
        vectors = jnp.concatenate(
            [g_vecs[...], vec_two[...]] + [bias[:, i * D : (i + 1) * D] for i in range(3)], axis=0
        )
        parts = ride.shape[0]
        width = D // parts
        for w in range(parts):
            ride[w, 0:9, 0:width] = vectors[:, w * width : (w + 1) * width]
        sums = jnp.sum(stats[...], axis=1, keepdims=True)
        tokens = lax.fori_loop(
            0, pl.num_programs(0), lambda w, total: total + lengths[w], jnp.int32(0)
        ).astype(F32)
        at = lane_iota(1, LANES)
        last = jnp.where(at == 3, tokens, 0.0)
        for i in range(3):
            last = jnp.where(at == i, sums[i : i + 1, :], last)
        mine = core[0]

        def group(i, carry):
            at = pl.multiple_of(i * 2 * rows, 2 * rows)
            block = a_qkv[pl.ds(at, 2 * rows), :]
            low, high = block[:rows], block[rows:]
            vecs = ride[2 * i // inner]
            for j, first, second in ((0, keep_first, keep_second), (1, send_first, send_second)):
                want = mine == j
                staging[:rows, :] = jnp.where(want, low, high)
                staging[rows : rows + 4, :LANES] = vecs[0:4]
                staging[rows : rows + 4, LANES : 2 * LANES] = vecs[4:8]
                staging[rows : rows + 1, 2 * LANES : 3 * LANES] = vecs[8:9]
                staging[rows + 1 : rows + 2, 2 * LANES : 2 * LANES + share] = jnp.where(
                    want, bias_up[2 * i], bias_up[2 * i + 1]
                )
                staging[rows + 2 : rows + 3, 2 * LANES : 3 * LANES] = last
                first[i] = staging[:, :cut].astype(BF16)
                second[i] = staging[:rows, cut:].astype(BF16)
            return carry

        lax.fori_loop(0, groups // 2, group, 0)


def rows_spec(*dims, count=1):
    rank = len(dims)
    return pl.BlockSpec((count,) + dims, lambda w, *_: (w,) + (0,) * rank)


def whole_spec(*dims):
    rank = len(dims)
    return pl.BlockSpec(dims, lambda w, *_: (0,) * rank, pipeline_mode=pl.Buffered(1))


def call(kernel, scalars, windows, in_specs, outs, scratch, name):
    return pl.pallas_call(
        kernel,
        out_shape=[jax.ShapeDtypeStruct(shape, dtype) for _, shape, dtype in outs],
        grid_spec=pltpu.PrefetchScalarGridSpec(
            num_scalar_prefetch=scalars,
            grid=(windows,),
            in_specs=in_specs,
            out_specs=[spec for spec, _, _ in outs],
            scratch_shapes=scratch,
        ),
        compiler_params=pltpu.CompilerParams(
            dimension_semantics=("arbitrary",), vmem_limit_bytes=63 * 1024 * 1024
        ),
        name=name,
    )


def flat_index():
    return lax.axis_index("wa") * lax.axis_size("an") + lax.axis_index("an")


def swap(value, bit, devices):
    return lax.ppermute(value, BOTH, [(i, i ^ (1 << bit)) for i in range(devices)])


def gather_steps(shards, orders, devices):
    index = flat_index()
    done = [[] for _ in shards]
    values = list(shards)
    for step in range(len(orders[0]) - 1):
        for i, order in enumerate(orders):
            bit = order[step]
            mine = values[i]
            other = swap(mine, bit, devices)
            low = ((index >> bit) & 1) == 0
            axis = sum(1 for b in done[i] if b > bit)
            values[i] = jnp.stack(
                [jnp.where(low, mine, other), jnp.where(low, other, mine)], axis=axis
            )
            done[i].append(bit)
    values = [v.reshape((devices // 2,) + s.shape) for v, s in zip(values, shards)]
    return [(v, swap(v, 0, devices)) for v in values]


def scatter_steps(halves, orders, devices):
    index = flat_index()
    bits = devices.bit_length() - 1
    left = [list(range(bits - 1, 0, -1)) for _ in halves]
    shape = (2,) * (bits - 1)
    values = []
    for keep, send in halves:
        got = swap(send, 0, devices)
        values.append((keep.reshape(shape + keep.shape[1:]), got.reshape(shape + keep.shape[1:])))
    for step in range(1, bits):
        for i, order in enumerate(orders):
            bit = order[step]
            axis = left[i].index(bit)
            own = (index >> bit) & 1

            def half(which):
                keep, got = (
                    lax.dynamic_index_in_dim(v, which, axis, keepdims=False).astype(F32)
                    for v in values[i]
                )
                return keep + got

            got = swap(half(1 - own).astype(BF16), bit, devices)
            values[i] = (half(own), got)
            left[i].remove(bit)
    return [keep + got.astype(F32) for keep, got in values]


def rotary_tables(positions):
    inverse = 10000.0 ** (-np.arange(0, HW, 2, dtype=np.float32) / np.float32(HW))
    inverse = jnp.asarray(np.tile(inverse.astype(np.float32), 2 * GROUP))
    angles = positions.astype(F32)[:, None] * inverse
    first = (lane_iota(1, LANES) % HW) < HW // 2
    return jnp.cos(angles), jnp.where(first, -1.0, 1.0) * jnp.sin(angles)


def body(
    span_states,
    offsets,
    lengths,
    cotangent,
    qkv_weight,
    out_weight,
    up_weight,
    down_weight,
    up_bias,
    norm_gains,
    norm_shifts,
    qkv_bias,
    out_biases,
):
    windows = span_states.shape[0]
    wa, an = lax.axis_size("wa"), lax.axis_size("an")
    devices = wa * an
    bits = devices.bit_length() - 1
    steps = FF // D
    even = D % (4 * devices) == 0 and devices == 1 << bits and an % 2 == 0
    rows = D // devices if even else 0
    cut = 8 * LANES
    share = D // wa
    up_share = FF // devices
    core = (flat_index() & 1).astype(jnp.int32)[None]
    small = jnp.concatenate([norm_gains, norm_shifts, qkv_bias, out_biases], axis=0)
    if rows:
        down_order = list(range(bits))[::-1]
        other_order = list(down_order)
        other_order[-2], other_order[-3] = other_order[-3], other_order[-2]
        shard = qkv_weight.reshape(rows, 3 * D)
        extra = jnp.concatenate([small.reshape(-1), up_bias])
        extra = jnp.pad(extra, (0, cut - extra.shape[0]))[None]
        (own_first, other_first), (own_second, other_second) = gather_steps(
            [jnp.concatenate([shard[:, :cut], extra], axis=0), shard[:, cut:]],
            [down_order, other_order],
            devices,
        )
        weights = [own_first, other_first, own_second, other_second]
        small = own_first[:: an // 2, rows, : 9 * share]
        small = small.reshape(wa, 9, share).transpose(1, 0, 2).reshape(9, D).astype(F32)
        ups = [v[:, rows, 9 * share : 9 * share + up_share] for v in (own_first, other_first)]
        low = core[0] == 0
        bias_up = jnp.stack(
            [jnp.where(low, ups[0], ups[1]), jnp.where(low, ups[1], ups[0])], axis=1
        )
        bias_up = bias_up.astype(F32).reshape(1, FF)
        up = up_weight.reshape(rows, steps, D).transpose(1, 0, 2).reshape(steps * rows, D)
        pack_rows = -(-(2 * steps + 1) * rows // 32) * 32
        pad = jnp.zeros((pack_rows - (2 * steps + 1) * rows, D), BF16)
        packed = jnp.concatenate([down_weight.reshape(-1, D), up, out_weight.reshape(-1, D), pad])
        packed = lax.all_gather(packed, BOTH, axis=0, tiled=False)
    else:
        w_qkv = lax.all_gather(qkv_weight, BOTH, axis=0, tiled=True).reshape(D, 3 * D)
        weights = [w_qkv]
        small = lax.all_gather(small, "wa", axis=1, tiled=True).astype(F32)
        bias_up = lax.all_gather(up_bias, BOTH, axis=0, tiled=True).astype(F32).reshape(1, FF)
        w_down = lax.all_gather(down_weight, BOTH, axis=0, tiled=True).reshape(FF, D)
        w_up = lax.all_gather(up_weight, BOTH, axis=0, tiled=True)
        w_up = w_up.reshape(D, steps, D).transpose(1, 0, 2).reshape(FF, D)
        w_out = lax.all_gather(out_weight, BOTH, axis=0, tiled=True).reshape(D, D)
        packed = jnp.concatenate([w_down, w_up, w_out], axis=0)
    cosine, sine = rotary_tables(jnp.arange(L, dtype=jnp.int32))
    offset_turns = jnp.stack(rotary_tables(offsets), axis=1)

    tiled_spec = rows_spec(TILES, L, LANES)
    tiled_shape = (windows, TILES, L, LANES)
    flat_spec = rows_spec(L, D)
    flat_shape = (windows, L, D)
    pair = 1
    tiled_pair = rows_spec(TILES, L, LANES, count=pair)
    flat_pair = rows_spec(L, D, count=pair)
    table_spec = whole_spec(L, LANES)
    turn_spec = rows_spec(2, LANES)

    tiled_out = (tiled_spec, tiled_shape, BF16)

    def kept(shape, dtype):
        return (whole_spec(*shape), shape, dtype)

    x, q, k, v, lse, mixed, w_qkv = call(
        functools.partial(front_kernel, rows),
        3,
        windows,
        [rows_spec(SPAN, D)]
        + [whole_spec(*w.shape) for w in weights]
        + [whole_spec(9, D), table_spec, table_spec, turn_spec],
        [(flat_spec, flat_shape, BF16)] + [tiled_out] * 5 + [kept((D, 3 * D), BF16)],
        [
            pltpu.VMEM((L, 3 * D), F32),
            pltpu.VMEM((GROUP * L, 2 * LANES), BF16),
            pltpu.VMEM((GROUP * L, 2 * LANES), BF16),
            pltpu.VMEM((max(4 * rows, 8), 3 * D), F32),
        ],
        "front",
    )(offsets, lengths, core, span_states, *weights, small, cosine, sine, offset_turns)

    activations, grad_mid, grad_mixed, dots, g_packed, g_vec_two, g_bias_up, stats = call(
        functools.partial(middle_kernel, rows),
        1,
        windows // pair,
        [
            flat_pair,
            tiled_pair,
            flat_pair,
            pl.BlockSpec(memory_space=pl.ANY),
            whole_spec(9, D),
            whole_spec(1, FF),
        ],
        [
            (flat_pair, flat_shape, BF16),
            (flat_pair, flat_shape, F32),
            (tiled_pair, tiled_shape, BF16),
            (tiled_pair, tiled_shape, BF16),
            kept(packed.shape, BF16),
            kept((4, D), F32),
            kept((1, FF), F32),
            kept((3, D), F32),
        ],
        [
            pltpu.VMEM((D, D), BF16),
            pltpu.VMEM((D, FF), BF16),
            pltpu.VMEM((FF, D), BF16),
            pltpu.VMEM((D, D), F32),
            pltpu.VMEM((D, FF), F32),
            pltpu.VMEM((FF, D), F32),
            pltpu.VMEM((packed.shape[1] if rows else 8, FF), F32),
            pltpu.SemaphoreType.DMA(()),
        ],
        "middle",
    )(lengths, x, mixed, cotangent, packed, small, bias_up)

    if rows:
        packed_shard = lax.psum_scatter(g_packed, BOTH, scatter_dimension=0, tiled=False)
        packed_shard = packed_shard.astype(F32)
        down_grad = packed_shard[: steps * rows].reshape(-1)
        up_grad = packed_shard[steps * rows : 2 * steps * rows].reshape(steps, rows, D)
        up_grad = up_grad.transpose(1, 0, 2).reshape(-1)
        out_grad = packed_shard[2 * steps * rows : (2 * steps + 1) * rows].reshape(-1)
    else:

        def scatter_flat(grad):
            flat = grad.reshape(devices, -1)
            return lax.psum_scatter(flat, BOTH, scatter_dimension=0, tiled=False).astype(F32)

        down_grad = scatter_flat(g_packed[:FF])
        g_up = g_packed[FF : 2 * FF].reshape(steps, D, D).transpose(1, 0, 2)
        up_grad = scatter_flat(g_up)
        out_grad = scatter_flat(g_packed[2 * FF :])

    half = devices // 2
    if rows:
        shape_first, shape_second = (half, rows + 4, cut), (half, rows, 3 * D - cut)
        halves = [shape_first, shape_first, shape_second, shape_second]
        bias_up_rows = g_bias_up.reshape(devices, 1, up_share)
    else:
        halves = [(D, 3 * D)] + [(8, LANES)] * 3
        bias_up_rows = jnp.zeros((devices, 1, up_share), F32)
    span_grad, *halves, g_vec_one, g_bias_qkv = call(
        functools.partial(back_kernel, rows, an),
        3,
        windows,
        [flat_spec]
        + [tiled_spec] * 6
        + [flat_spec, whole_spec(D, 3 * D), whole_spec(9, D), table_spec, table_spec, turn_spec]
        + [whole_spec(4, D), whole_spec(devices, 1, up_share), whole_spec(3, D)],
        [(rows_spec(SPAN, D), (windows, SPAN, D), BF16)]
        + [kept(shape, BF16) for shape in halves]
        + [kept((2, D), F32), kept((1, 3 * D), F32)],
        [
            pltpu.VMEM((D, 3 * D), F32),
            pltpu.VMEM((L, 3 * D), BF16),
            pltpu.VMEM((GROUP * L, 2 * LANES), BF16),
            pltpu.VMEM((GROUP * L, 2 * LANES), BF16),
            pltpu.VMEM((L, GROUP * L), BF16),
            pltpu.VMEM((wa if rows else 1, 16, LANES), F32),
            pltpu.VMEM((rows + 4, 3 * D), F32),
        ],
        "back",
    )(
        offsets, lengths, core, x, q, k, v, lse, grad_mixed, dots, grad_mid, w_qkv, small,
        cosine, sine, offset_turns, g_vec_two, bias_up_rows, stats,
    )

    if rows:
        g_first, g_second = scatter_steps(
            [halves[:2], halves[2:]], [down_order[::-1], other_order[::-1]], devices
        )
        qkv_grad = jnp.concatenate([g_first[:rows], g_second], axis=1).reshape(-1)
        ride = g_first[rows:]
        third = ride[:, 2 * LANES : 3 * LANES]
        shares = jnp.concatenate(
            [ride[:, :share], ride[:, LANES : LANES + share], third[:1, :share]], axis=0
        )
        up_bias_grad = third[1, :up_share]
        totals = third[2, :4]
    else:
        qkv_grad = scatter_flat(halves[0])
        token_count = jnp.sum(lengths).astype(F32)
        totals = jnp.concatenate([jnp.sum(stats, axis=1), token_count[None]])
        vec_sums = jnp.concatenate([g_vec_one, g_vec_two, g_bias_qkv.reshape(3, D)], axis=0)
        vec_sums, up_sums, totals = lax.psum((vec_sums, g_bias_up.reshape(FF), totals), BOTH)
        shares = lax.dynamic_slice_in_dim(vec_sums, lax.axis_index("wa") * share, share, 1)
        up_bias_grad = lax.dynamic_slice_in_dim(up_sums, flat_index() * up_share, up_share, 0)
    root_means = jnp.sqrt(totals[:3] / (totals[3] * D))
    return (
        activations,
        span_grad,
        qkv_grad,
        out_grad,
        up_grad,
        down_grad,
        up_bias_grad,
        jnp.stack([shares[0], shares[2]]),
        jnp.stack([shares[1], shares[3]]),
        shares[6:9],
        shares[4:6],
        root_means,
    )


def solution(mesh):
    return jax.shard_map(
        body,
        mesh=mesh,
        in_specs=(
            P(("wa", "an"), None, None),
            P(("wa", "an")),
            P(("wa", "an")),
            P(("wa", "an"), None, None),
            P(("wa", "an")),
            P(("wa", "an")),
            P(("wa", "an")),
            P(("wa", "an")),
            P(("wa", "an")),
            P(None, "wa"),
            P(None, "wa"),
            P(None, "wa"),
            P(None, "wa"),
        ),
        out_specs=(
            P(("wa", "an"), None, None),
            P(("wa", "an"), None, None),
            P(("wa", "an")),
            P(("wa", "an")),
            P(("wa", "an")),
            P(("wa", "an")),
            P(("wa", "an")),
            P(None, "wa"),
            P(None, "wa"),
            P(None, "wa"),
            P(None, "wa"),
            P(),
        ),
        check_vma=False,
    )
```
